512 devices in a mesh: dp: 32 (over x, z_hi, core), tensor: 16 (over y, z_lo).
Axes of the slice: x: 4, y: 4, z: 16 (z_hi: 4, z_lo: 4; z = z_hi * 4 + z_lo), core: 2. Of those that a mesh axis runs over, the one named last changes fastest.
Arguments:
- rm_hidden: bfloat16 [32, 1024, 3584], P('dp', 'tensor'), may hold values from -6 to 6
- rm_cotangent: bfloat16 [32, 1024, 3584], P('dp', 'tensor'), may hold values from -6 to 6
- rm_gain: float32 [3584], replicated, may hold values from 0.25 to 1.75
- rewards: float32 [32], P('dp'), may hold values from 0.25 to 8, as said below
- visual_pos: int32 [32, 512], P('dp', 'tensor'), may hold values from 0 to 1023, as said below
- bridge: bfloat16 [3584, 2048], P(None, 'tensor'), may hold values from -0.09375 to 0.09375
- img_query: bfloat16 [32, 2048, 2048], P('dp', 'tensor'), may hold values from -8 to 8
- img_key: bfloat16 [32, 2048, 2048], P('dp', 'tensor'), may hold values from -8 to 8
- img_value: bfloat16 [32, 2048, 2048], P('dp', 'tensor'), may hold values from -6 to 6
Outputs:
- grad_query: bfloat16 [32, 2048, 2048], P('dp', 'tensor')
- grad_key: bfloat16 [32, 2048, 2048], P('dp', 'tensor')
- grad_value: bfloat16 [32, 2048, 2048], P('dp', 'tensor')
The draws below stay inside these ranges and needn't reach their ends.
Inputs may be any that keep to these rules, and one draw needn't show every extreme that they name: `visual_pos`: strictly increasing in each sample; rows 64 * t to 64 * t + 63 of a reward sequence hold exactly 32 visual tokens, for every t. `rewards`: positive.
All inputs are finite; a program needn't handle non-finite values.
Results may differ from the reference program's by a relative error of at most 0.0082.
Values may be sent and summed in bfloat16 or wider, within the bound.
A program may use at most 64 MiB of HBM per device.

```python
import jax
import jax.numpy as jnp
from jax import lax

D = 3584
HEADS = 16
HD = 128
GW = 64
SAMPLES = 32
L = 2048
HW = 2048
VIS = 512
VIS_DEV = 32
RM_DEV = 64
RSEQ = 1024


def draw_rewards(key, part):
    index_f = jnp.arange(SAMPLES, dtype=jnp.float32)
    ramp = 3.0 ** (index_f / max(SAMPLES - 1, 1))
    noise = jnp.exp(jax.random.uniform(key, (SAMPLES,), jnp.float32, jnp.log(0.6), jnp.log(1.6)))
    return (ramp * noise).astype(jnp.float32)


def draw_visual_pos(key, part):
    blocks = VIS // VIS_DEV
    random_ints = jax.random.randint(key, (SAMPLES, blocks, RM_DEV), 0, 2 ** 20)
    scores = random_ints * RM_DEV + jnp.arange(RM_DEV, dtype=jnp.int32)
    permuted = jnp.argsort(scores, axis=-1)
    picked = jnp.sort(permuted[:, :, :VIS_DEV], axis=-1)
    block_start = jnp.arange(blocks, dtype=jnp.int32)[None, :, None] * RM_DEV
    return (picked + block_start).reshape(SAMPLES, VIS).astype(jnp.int32)


def drawn_pair(key):
    shape = (SAMPLES, L, HEADS * HD)
    query_draw = jnp.clip(jax.random.normal(jax.random.fold_in(key, 101), shape, jnp.float32), -8.0, 8.0)
    key_draw = jnp.clip(jax.random.normal(jax.random.fold_in(key, 102), shape, jnp.float32), -8.0, 8.0)
    return (query_draw, key_draw)


def draw_img_query(key, part):
    return drawn_pair(key)[0].astype(jnp.bfloat16)


def draw_img_key(key, part):
    return drawn_pair(key)[1].astype(jnp.bfloat16)


def steps_of(own_key, extent, split, smallest, largest):
    level = 1.0
    for axis_at, shards_of in split:
        steps = jax.random.uniform(jax.random.fold_in(jax.random.fold_in(own_key, 6), axis_at), (shards_of,), jnp.float32, smallest / len(split), largest / len(split))
        level = level * jnp.repeat(jnp.exp(steps), extent[axis_at] // shards_of).reshape((-1,) + (1,) * (len(extent) - 1 - axis_at))
    return level


def bell_draw(own_key, extent, width, reach, pieces=(), kind=jnp.bfloat16):
    values = jax.random.normal(own_key, extent, jnp.float32) * width
    if len(pieces) > 0:
        values = steps_of(own_key, extent, pieces, -0.22, 0.18) * values
    return jnp.clip(values, min=-reach, max=reach).astype(kind)


def setup_inputs(seed: int = 0) -> dict:
    arg_keys = jax.random.split(jax.random.key(seed), 10)
    rm_hidden = bell_draw(arg_keys[0], (SAMPLES, RSEQ, D), 1.0, 6.0, ((0, 32), (1, 16)))
    rm_cotangent = bell_draw(arg_keys[1], (SAMPLES, RSEQ, D), 1.0, 6.0, ((0, 32), (1, 16)))
    rm_gain = jnp.clip(1.0 + 0.15 * jax.random.normal(arg_keys[2], (D,), jnp.float32), 0.25, 1.75)
    rewards = draw_rewards(jax.random.fold_in(arg_keys[9], 71), 0)
    visual_pos = draw_visual_pos(jax.random.fold_in(arg_keys[9], 71), 0)
    bridge = bell_draw(arg_keys[5], (D, HW), D ** -0.5, 0.09375, ((1, 16),))
    img_query = draw_img_query(jax.random.fold_in(arg_keys[9], 71), 0)
    img_key = draw_img_key(jax.random.fold_in(arg_keys[9], 71), 0)
    img_value = bell_draw(arg_keys[8], (SAMPLES, L, HW), 1.0, 6.0, ((0, 32), (1, 16)))
    return dict(rm_hidden=rm_hidden, rm_cotangent=rm_cotangent, rm_gain=rm_gain, rewards=rewards, visual_pos=visual_pos, bridge=bridge, img_query=img_query, img_key=img_key, img_value=img_value)


def norm_backward(hidden, cotangent, gain):
    hidden_f = hidden.astype(jnp.float32)
    scaled_cot = cotangent.astype(jnp.float32) * gain.astype(jnp.float32)
    inv_rms = lax.rsqrt(lax.optimization_barrier(jnp.mean(hidden_f * hidden_f, axis=-1, keepdims=True)) + 1e-06)
    mixed = lax.optimization_barrier(jnp.mean(hidden_f * scaled_cot, axis=-1, keepdims=True))
    return (inv_rms * scaled_cot - hidden_f * inv_rms * inv_rms * inv_rms * mixed).astype(jnp.bfloat16)

def upsample(handed):
    half_width = GW // 2
    grid_rows = handed.reshape(handed.shape[0] // half_width, half_width, handed.shape[1])
    grid_rows = jnp.repeat(jnp.repeat(grid_rows, 2, axis=0), 2, axis=1)
    return grid_rows.reshape(-1, handed.shape[1])

def attend_back(query_rows, key_rows, value_rows, grad_rows):
    seq_length = query_rows.shape[0]
    block_rows = min(512, seq_length)
    score_scale = query_rows.shape[1] ** (-0.5)

    def step(carry, block_index):
        grad_key, grad_value = carry
        first_row = (block_index * block_rows).astype(jnp.int32)
        query_block = lax.dynamic_slice_in_dim(query_rows, first_row, block_rows, 0)
        grad_block = lax.dynamic_slice_in_dim(grad_rows, first_row, block_rows, 0)
        scores = jnp.dot(query_block, key_rows.T, preferred_element_type=jnp.float32) * score_scale
        row_max = lax.optimization_barrier(jnp.max(scores, axis=1, keepdims=True))
        exp_scores = jnp.exp(scores - row_max)
        attn_weights = exp_scores / lax.optimization_barrier(jnp.sum(exp_scores, axis=1, keepdims=True))
        weights_half = attn_weights.astype(jnp.bfloat16)
        grad_weights = jnp.dot(grad_block, value_rows.T, preferred_element_type=jnp.float32)
        row_dot = lax.optimization_barrier(jnp.sum(attn_weights * grad_weights, axis=1, keepdims=True))
        grad_scores = (attn_weights * (grad_weights - row_dot)).astype(jnp.bfloat16)
        grad_query = (jnp.dot(grad_scores, key_rows, preferred_element_type=jnp.float32) * score_scale).astype(jnp.bfloat16)
        grad_key = grad_key + jnp.dot(grad_scores.T, query_block, preferred_element_type=jnp.float32)
        grad_value = grad_value + jnp.dot(weights_half.T, grad_block, preferred_element_type=jnp.float32)
        return ((grad_key, grad_value), grad_query)
    zeros_init = jnp.zeros(query_rows.shape, jnp.float32)
    carry, query_blocks = lax.scan(step, (zeros_init, zeros_init), jnp.arange(seq_length // block_rows, dtype=jnp.int32))
    grad_query = query_blocks.reshape(seq_length, -1)
    grad_key = (carry[0] * score_scale).astype(jnp.bfloat16)
    grad_value = carry[1].astype(jnp.bfloat16)
    return (grad_query, grad_key, grad_value)

def heads_backward(query_rows, key_rows, value_rows, grad_rows):
    seq_length = query_rows.shape[0]
    head_count = query_rows.shape[1] // HD

    def split_heads(array):
        return array.reshape(seq_length, head_count, HD).transpose(1, 0, 2)

    def per_head(head_items):
        return attend_back(head_items[0], head_items[1], head_items[2], head_items[3])
    head_grads = lax.map(per_head, (split_heads(query_rows), split_heads(key_rows), split_heads(value_rows), split_heads(grad_rows)))
    return tuple((grads.transpose(1, 0, 2).reshape(seq_length, head_count * HD) for grads in head_grads))

def reference(rm_hidden, rm_cotangent, rm_gain, rewards, visual_pos, bridge, img_query, img_key, img_value):
    reward_weight = rewards * SAMPLES / jnp.sum(rewards)

    def per_sample(sample_items):
        hidden, cotangent, positions, weight, query_rows, key_rows, value_rows = sample_items
        vis_hidden = jnp.take(hidden, positions.astype(jnp.int32), axis=0)
        vis_cot = jnp.take(cotangent, positions.astype(jnp.int32), axis=0)
        visual_grad = norm_backward(vis_hidden, vis_cot, rm_gain)
        handed = (jnp.dot(visual_grad, bridge, preferred_element_type=jnp.float32) * weight).astype(jnp.bfloat16)
        grad_rows = upsample(handed)
        return heads_backward(query_rows, key_rows, value_rows, grad_rows)
    outputs = lax.map(per_sample, (rm_hidden, rm_cotangent, visual_pos, reward_weight, img_query, img_key, img_value))
    return (outputs[0], outputs[1], outputs[2])
```

```python
import functools
from typing import NamedTuple, Any

import jax
import jax.numpy as jnp
from jax import lax
from jax.experimental import pallas as pl
from jax.experimental.pallas import tpu as pltpu
from jax.sharding import Mesh
from jax.sharding import PartitionSpec as P

HD = 128
GW = 64
D = 3584
DP = ("dp_0", "dp_1", "dp_2")
SEQ = 2048
VIS = 512
TP = 16
NY, NZ = 4, 4
QB = 512
UB = QB // 4
KC = 256
SCALE = HD**-0.5
LOG2E = 1.4426950408889634
BF = jnp.bfloat16
F32 = jnp.float32

NT = (((1,), (1,)), ((), ()))
NN = (((1,), (0,)), ((), ()))
TN = (((0,), (0,)), ((), ()))


def mm(a, b, dims=NN):
    return lax.dot_general(a, b, dims, preferred_element_type=F32)


class AttnScratch(NamedTuple):
    s_buf: Any
    dp_buf: Any
    perm: Any
    perm_t: Any
    k_t: Any
    dq_t: Any
    dk_acc: Any
    dv_acc: Any


def attn_scratch():
    return [
        pltpu.VMEM((SEQ, QB), F32),
        pltpu.VMEM((SEQ, UB), F32),
        pltpu.VMEM((QB, QB), BF),
        pltpu.VMEM((QB, QB), BF),
        pltpu.VMEM((HD, SEQ), BF),
        pltpu.VMEM((HD, QB), F32),
        pltpu.VMEM((SEQ, HD), F32),
        pltpu.VMEM((SEQ, HD), F32),
    ]


def grouped(rank):
    group, place = rank // UB, rank % UB
    return (place // 32) * HD + (group // 2) * GW + 2 * (place % 32) + group % 2


def attn_tables(env):
    row = lax.broadcasted_iota(jnp.int32, (QB, QB), 0)
    col = lax.broadcasted_iota(jnp.int32, (QB, QB), 1)
    env.perm[...] = (grouped(row) == col).astype(F32).astype(BF)
    env.perm_t[...] = (grouped(col) == row).astype(F32).astype(BF)
    env.dk_acc[...] = jnp.zeros((SEQ, HD), F32)
    env.dv_acc[...] = jnp.zeros((SEQ, HD), F32)


def attn_transpose(env, k_all):
    eye = (
        lax.broadcasted_iota(jnp.int32, (HD, HD), 0)
        == lax.broadcasted_iota(jnp.int32, (HD, HD), 1)
    ).astype(F32).astype(BF)
    env.k_t[...] = mm(eye, k_all[...], NT).astype(BF)


def attn_setup(env, k_all):
    attn_tables(env)
    attn_transpose(env, k_all)


def fold(values, op):
    return op(values.reshape(values.shape[0] // 8, 8, values.shape[1]), axis=0)


def four(values):
    return jnp.concatenate([values] * 4, axis=1)


def attn_block(env, block, q_all, k_all, v_all, hand_all, dq_all):
    q_rows = pl.ds(pl.multiple_of(block * QB, QB), QB)
    q_g = mm(env.perm[...], q_all[q_rows, :]).astype(BF)
    hand = hand_all[pl.ds(pl.multiple_of(block * UB, UB), UB), :]

    def rows(chunk):
        return pl.ds(pl.multiple_of(chunk * KC, KC), KC)

    def scores(chunk, top):
        s = mm(k_all[rows(chunk), :], q_g, NT)
        env.s_buf[rows(chunk), :] = s
        return jnp.maximum(top, fold(s, jnp.max))

    top = lax.fori_loop(0, SEQ // KC, scores, jnp.full((8, QB), -jnp.inf, F32), unroll=2)
    top = jnp.max(top, axis=0, keepdims=True)

    def weights(chunk, carry):
        total, dot_sum = carry
        e = jnp.exp2((env.s_buf[rows(chunk), :] - top) * (SCALE * LOG2E))
        env.s_buf[rows(chunk), :] = e
        dp = mm(v_all[rows(chunk), :], hand, NT)
        env.dp_buf[rows(chunk), :] = dp
        return total + fold(e, jnp.sum), dot_sum + fold(e * four(dp), jnp.sum)

    zeros = jnp.zeros((8, QB), F32)
    total, dot_sum = lax.fori_loop(0, SEQ // KC, weights, (zeros, zeros), unroll=2)
    inv = 1.0 / jnp.sum(total, axis=0, keepdims=True)
    row_dot = jnp.sum(dot_sum, axis=0, keepdims=True) * inv
    env.dq_t[...] = jnp.zeros((HD, QB), F32)

    def grads(chunk, _):
        p = env.s_buf[rows(chunk), :] * inv
        ds = (p * (four(env.dp_buf[rows(chunk), :]) - row_dot)).astype(BF)
        p_sum = (p[:, :UB] + p[:, UB : 2 * UB]) + (p[:, 2 * UB : 3 * UB] + p[:, 3 * UB :])
        env.dk_acc[rows(chunk), :] += mm(ds, q_g)
        env.dv_acc[rows(chunk), :] += mm(p_sum.astype(BF), hand)
        env.dq_t[...] += mm(env.k_t[:, rows(chunk)], ds)
        return 0

    lax.fori_loop(0, SEQ // KC, grads, 0, unroll=2)
    dq_t = (env.dq_t[...] * SCALE).astype(BF)
    dq_all[q_rows, :] = mm(env.perm_t[...], dq_t, NT).astype(BF)


def attn_finish(env, dk_all, dv_all):
    dk_all[...] = (env.dk_acc[...] * SCALE).astype(BF)
    dv_all[...] = env.dv_acc[...].astype(BF)


class Links(NamedTuple):
    x: Any
    z_hi: Any
    core: Any
    tensor: Any
    sizes: tuple


def remote(src, dst, send_sem, recv_sem, device):
    return pltpu.make_async_remote_copy(
        src_ref=src,
        dst_ref=dst,
        send_sem=send_sem,
        recv_sem=recv_sem,
        device_id=device,
        device_id_type=pl.DeviceIdType.MESH,
    )


def kernel(
    sizes,
    rew_ref,
    pos_ref,
    gain_ref,
    hid_hbm,
    cot_hbm,
    bridge_hbm,
    q_hbm,
    k_hbm,
    v_hbm,
    dq_out,
    dk_out,
    dv_out,
    hid,
    cot,
    vg_all,
    bridge_all,
    hand_mine,
    hand_all,
    q_all,
    k_all,
    v_all,
    dq_all,
    dk_all,
    dv_all,
    rew,
    own_sem,
    rew_send,
    rew_recv,
    vg_send,
    vg_recv,
    br_send,
    br_recv,
    hand_send,
    hand_recv,
    q_send,
    q_recv,
    k_send,
    k_recv,
    v_send,
    v_recv,
    dq_send,
    dq_recv,
    dk_send,
    dk_recv,
    dv_send,
    dv_recv,
    *scratch,
):
    env = AttnScratch(*scratch)
    n_x, n_zhi, n_core = sizes
    x, z_hi, core, me = (lax.axis_index(a) for a in (*DP, "tensor"))
    y, z = me // NZ, me % NZ
    axis_of = {"dp_0": (x, n_x), "dp_1": (z_hi, n_zhi), "dp_2": (core, n_core)}

    def turned(name, step):
        place, size = axis_of[name]
        return {name: lax.rem(place + step, size)}

    barrier = pltpu.get_barrier_semaphore()

    def greet(step, _):
        pl.semaphore_signal(
            barrier,
            inc=1,
            device_id={"tensor": lax.rem(me + step, TP)},
            device_id_type=pl.DeviceIdType.MESH,
        )
        return 0

    lax.fori_loop(1, TP, greet, 0)
    partners = TP - 1
    for name, (_, size) in axis_of.items():
        for step in range(1, size):
            pl.semaphore_signal(
                barrier, inc=1, device_id=turned(name, step), device_id_type=pl.DeviceIdType.MESH
            )
            partners += 1

    mine = pl.ds(pl.multiple_of(me * HD, HD), HD)
    my_cols = pl.ds(pl.multiple_of(y * HD, HD), HD)
    local = [
        pltpu.make_async_copy(hid_hbm, hid, own_sem.at[0]),
        pltpu.make_async_copy(cot_hbm, cot, own_sem.at[1]),
        pltpu.make_async_copy(bridge_hbm, bridge_all.at[:, my_cols], own_sem.at[2]),
        pltpu.make_async_copy(k_hbm.at[:, mine], k_all.at[mine, :], own_sem.at[3]),
        pltpu.make_async_copy(v_hbm.at[:, mine], v_all.at[mine, :], own_sem.at[4]),
        pltpu.make_async_copy(q_hbm.at[:, mine], q_all.at[mine, :], own_sem.at[5]),
    ]
    for copy in local:
        copy.start()
    pl.semaphore_wait(barrier, partners)

    def reward_copies(first, name):
        place, size = axis_of[name]
        return [
            remote(
                rew.at[first + place],
                rew.at[first + place],
                rew_send.at[first + step],
                rew_recv.at[first + place],
                turned(name, step),
            )
            for step in range(1, size)
        ]

    def reward_start(first, name, value):
        rew[first + axis_of[name][0]] = value
        for copy in reward_copies(first, name):
            copy.start()

    def reward_sum(first, name):
        place, size = axis_of[name]
        for step in range(1, size):
            other = lax.rem(place + step, size)
            remote(
                rew.at[first + other],
                rew.at[first + other],
                rew_send.at[first + step],
                rew_recv.at[first + other],
                turned(name, step),
            ).wait_recv()
        total = rew[first]
        for slot in range(1, size):
            total = total + rew[first + slot]
        return total

    my_reward = jnp.full((8, HD), rew_ref[0], F32)
    reward_start(0, "dp_2", my_reward)

    half, quarter = D // 2, D // 4
    up, down = {"tensor": lax.rem(y + 1, NY) * NZ + z}, {"tensor": lax.rem(y + NY - 1, NY) * NZ + z}

    def bridge_region(owner, first, count):
        return bridge_all.at[
            pl.ds(pl.multiple_of(first, 16), count),
            pl.ds(pl.multiple_of(owner * HD, HD), HD),
        ]

    def bridge_own(device, slot):
        rows = pl.ds(pl.multiple_of(core * half, 16), half)
        return remote(
            bridge_hbm.at[rows, :],
            bridge_region(y, core * half, half),
            br_send.at[slot],
            br_recv.at[slot],
            device,
        )

    def bridge_copy(owner, first, count, slot, device):
        region = bridge_region(owner, first, count)
        return remote(region, region, br_send.at[slot], br_recv.at[slot], device)

    below, above = lax.rem(y + NY - 1, NY), lax.rem(y + 1, NY)
    across = lax.rem(y + 2, NY)
    bridge_up, bridge_down = bridge_own(up, 0), bridge_own(down, 1)
    bridge_up.start()
    bridge_down.start()

    def peer_at(step):
        d_y, d_z = step // NZ, step % NZ
        return lax.rem(y - d_y + NY, NY) * NZ + lax.rem(z + d_z, NZ)

    def head_send(array, all_ref, sends, recvs, peer):
        cols = pl.ds(pl.multiple_of(peer * HD, HD), HD)
        return remote(
            array.at[:, cols], all_ref.at[mine, :], sends.at[peer], recvs.at[me], {"tensor": peer}
        )

    def head_recv(all_ref, sends, recvs, peer):
        region = all_ref.at[pl.ds(pl.multiple_of(peer * HD, HD), HD), :]
        return remote(region, region, sends.at[peer], recvs.at[peer], {"tensor": peer})

    def to_all(copy_to):
        def one(step, _):
            copy_to(peer_at(step))
            return 0

        lax.fori_loop(1, TP, one, 0)

    to_all(lambda peer: head_send(k_hbm, k_all, k_send, k_recv, peer).start())

    local[0].wait()
    local[1].wait()
    local_rows = pos_ref[...] - me * hid.shape[0]
    picked = (
        lax.broadcasted_iota(jnp.int32, (hid.shape[0], local_rows.shape[1]), 0) == local_rows
    )
    picked = picked.astype(F32).astype(BF)
    hidden = mm(picked, hid[...], TN)
    scaled = mm(picked, cot[...], TN) * gain_ref[...]
    inv_rms = lax.rsqrt(jnp.mean(hidden * hidden, axis=-1, keepdims=True) + 1e-06)
    mixed = jnp.mean(hidden * scaled, axis=-1, keepdims=True)
    count = local_rows.shape[1]
    vg_all[pl.ds(pl.multiple_of(z * count, count), count), :] = (
        inv_rms * scaled - hidden * (inv_rms * inv_rms * inv_rms * mixed)
    ).astype(BF)

    def vg_copy(owner, slot, device):
        region = vg_all.at[pl.ds(pl.multiple_of(owner * count, count), count), :]
        return remote(region, region, vg_send.at[slot], vg_recv.at[slot], device)

    right = {"tensor": y * NZ + lax.rem(z + 1, NZ)}
    left = {"tensor": y * NZ + lax.rem(z + NZ - 1, NZ)}

    def vg_hop(hop, action):
        @pl.when((z < NZ - 1) & (z >= hop))
        def _():
            action(vg_copy(lax.rem(z - hop + NZ, NZ), hop, right))

        @pl.when((z > 0) & (z + hop < NZ))
        def _():
            action(vg_copy(lax.rem(z + hop, NZ), NZ + hop, left))

    def vg_take(hop):
        @pl.when(z > hop)
        def _():
            vg_copy(lax.rem(z - hop - 1 + NZ, NZ), hop, left).wait_recv()

        @pl.when(z + hop + 1 < NZ)
        def _():
            vg_copy(lax.rem(z + hop + 1, NZ), NZ + hop, right).wait_recv()

    vg_hop(0, lambda copy: copy.start())
    to_all(lambda peer: head_send(v_hbm, v_all, v_send, v_recv, peer).start())
    core_total = reward_sum(0, "dp_2")
    reward_start(2, "dp_0", core_total)
    attn_tables(env)

    vg_take(0)
    vg_hop(1, lambda copy: copy.start())
    to_all(lambda peer: head_send(q_hbm, q_all, q_send, q_recv, peer).start())
    x_total = reward_sum(2, "dp_0")
    reward_start(2 + 4, "dp_1", x_total)

    sibling = turned("dp_2", 1)
    bridge_copy(below, core * half, half, 0, down).wait_recv()
    on_up = bridge_copy(below, core * half, quarter, 2, up)
    on_up.start()
    share_below = bridge_copy(below, core * half, half, 4, sibling)
    share_below.start()
    bridge_copy(above, core * half, half, 1, up).wait_recv()
    on_down = bridge_copy(above, core * half + quarter, quarter, 3, down)
    on_down.start()
    share_above = bridge_copy(above, core * half, half, 5, sibling)
    share_above.start()
    vg_take(1)
    vg_hop(2, lambda copy: copy.start())
    bridge_copy(across, core * half, quarter, 2, down).wait_recv()
    bridge_copy(across, core * half + quarter, quarter, 3, up).wait_recv()
    share_across = bridge_copy(across, core * half, half, 6, sibling)
    share_across.start()
    other = (1 - core) * half
    vg_take(2)
    z_total = reward_sum(2 + 4, "dp_1")
    weight = rew_ref[0] * (n_x * n_zhi * n_core) / z_total[0:1, :]

    def hand_head(owner):
        cols = pl.ds(pl.multiple_of(owner * HD, HD), HD)
        product = mm(vg_all[...], bridge_all[:, cols])
        return (product * weight).astype(BF)

    my_rows = pl.ds(pl.multiple_of(y * UB, UB), UB)

    def hand_copy(step):
        head = lax.rem(y + step, NY)
        return remote(
            hand_mine.at[step],
            hand_all.at[my_rows, :],
            hand_send.at[step],
            hand_recv.at[y],
            {"tensor": head * NZ + z},
        )

    local[2].wait()
    hand_all[my_rows, :] = hand_head(y)
    for step, slot in ((1, 5), (3, 4), (2, 6)):
        owner = lax.rem(y + step, NY)
        bridge_copy(owner, other, half, slot, sibling).wait_recv()
        hand_mine[step] = hand_head(owner)
        hand_copy(step).start()

    for copy in local[3:]:
        copy.wait()
    to_all(lambda peer: head_recv(k_all, k_send, k_recv, peer).wait_recv())
    attn_transpose(env, k_all)
    to_all(lambda peer: head_recv(v_all, v_send, v_recv, peer).wait_recv())
    for step in range(1, NY):
        src = lax.rem(y + step, NY)
        region = hand_all.at[pl.ds(pl.multiple_of(src * UB, UB), UB), :]
        remote(
            region, region, hand_send.at[step], hand_recv.at[src], {"tensor": src * NZ + z}
        ).wait_recv()

    def token_send(all_ref, out, sends, recvs, peer):
        rows = pl.ds(pl.multiple_of(peer * HD, HD), HD)
        return remote(
            all_ref.at[rows, :], out.at[:, mine], sends.at[peer], recvs.at[me], {"tensor": peer}
        )

    def token_recv(out, sends, recvs, peer):
        region = out.at[:, pl.ds(pl.multiple_of(peer * HD, HD), HD)]
        return remote(region, region, sends.at[peer], recvs.at[peer], {"tensor": peer})

    def token_own(all_ref, out, slot):
        return pltpu.make_async_copy(all_ref.at[mine, :], out.at[:, mine], own_sem.at[slot])

    def attend(step, _):
        block = lax.rem(y + step, NY)

        def take(i, _):
            peer = block * NZ + i

            @pl.when(peer != me)
            def _():
                head_recv(q_all, q_send, q_recv, peer).wait_recv()

            return 0

        lax.fori_loop(0, NZ, take, 0)
        attn_block(env, block, q_all, k_all, v_all, hand_all, dq_all)

        def give(i, _):
            peer = block * NZ + lax.rem(z + i, NZ)

            @pl.when(peer != me)
            def _():
                token_send(dq_all, dq_out, dq_send, dq_recv, peer).start()

            return 0

        lax.fori_loop(0, NZ, give, 0)
        return 0

    lax.fori_loop(0, NY, attend, 0)
    attn_finish(env, dk_all, dv_all)
    to_all(lambda peer: token_send(dk_all, dk_out, dk_send, dk_recv, peer).start())
    to_all(lambda peer: token_send(dv_all, dv_out, dv_send, dv_recv, peer).start())
    own = [
        token_own(dq_all, dq_out, 0),
        token_own(dk_all, dk_out, 1),
        token_own(dv_all, dv_out, 2),
    ]
    for copy in own:
        copy.start()

    for first, name in ((0, "dp_2"), (2, "dp_0"), (2 + 4, "dp_1")):
        for copy in reward_copies(first, name):
            copy.wait_send()
    for copy in (bridge_up, bridge_down, on_up, on_down, share_below, share_above, share_across):
        copy.wait_send()
    for hop in range(NZ - 1):
        vg_hop(hop, lambda copy: copy.wait_send())
    for step in range(1, NY):
        hand_copy(step).wait_send()

    def settle(peer):
        head_send(k_hbm, k_all, k_send, k_recv, peer).wait_send()
        head_send(v_hbm, v_all, v_send, v_recv, peer).wait_send()
        head_send(q_hbm, q_all, q_send, q_recv, peer).wait_send()
        token_send(dq_all, dq_out, dq_send, dq_recv, peer).wait_send()
        token_send(dk_all, dk_out, dk_send, dk_recv, peer).wait_send()
        token_send(dv_all, dv_out, dv_send, dv_recv, peer).wait_send()
        token_recv(dq_out, dq_send, dq_recv, peer).wait_recv()
        token_recv(dk_out, dk_send, dk_recv, peer).wait_recv()
        token_recv(dv_out, dv_send, dv_recv, peer).wait_recv()

    to_all(settle)
    for copy in own:
        copy.wait()


def local(
    rm_hidden, rm_cotangent, rm_gain, rewards, visual_pos, bridge, img_query, img_key, img_value
):
    sizes = tuple(lax.axis_size(a) for a in DP)
    rows, depth = rm_hidden.shape[1:]
    count = visual_pos.shape[1]
    tokens = jax.ShapeDtypeStruct(img_query.shape[1:], BF)
    anywhere = pl.BlockSpec(memory_space=pl.ANY)
    in_vmem = pl.BlockSpec(memory_space=pltpu.VMEM)
    group = pltpu.SemaphoreType.DMA((TP,))
    head = pltpu.VMEM((SEQ, HD), BF)
    grads = pl.pallas_call(
        functools.partial(kernel, sizes),
        out_shape=[tokens] * 3,
        in_specs=[pl.BlockSpec(memory_space=pltpu.SMEM), in_vmem, in_vmem] + [anywhere] * 6,
        out_specs=[anywhere] * 3,
        scratch_shapes=[
            pltpu.VMEM((rows, depth), BF),
            pltpu.VMEM((rows, depth), BF),
            pltpu.VMEM((NZ * count, depth), BF),
            pltpu.VMEM((depth, NY * HD), BF),
            pltpu.VMEM((NY, UB, HD), BF),
            pltpu.VMEM((VIS, HD), BF),
            *([head] * 6),
            pltpu.VMEM((2 + 4 + 4, 8, HD), F32),
            pltpu.SemaphoreType.DMA((6,)),
            pltpu.SemaphoreType.DMA((10,)),
            pltpu.SemaphoreType.DMA((10,)),
            pltpu.SemaphoreType.DMA((2 * NZ,)),
            pltpu.SemaphoreType.DMA((2 * NZ,)),
            pltpu.SemaphoreType.DMA((7,)),
            pltpu.SemaphoreType.DMA((7,)),
            pltpu.SemaphoreType.DMA((NY,)),
            pltpu.SemaphoreType.DMA((NY,)),
            *([group] * 12),
            *attn_scratch(),
        ],
        compiler_params=pltpu.CompilerParams(
            collective_id=0, has_side_effects=True, vmem_limit_bytes=48 << 20
        ),
    )(
        rewards,
        visual_pos,
        rm_gain[None],
        rm_hidden[0],
        rm_cotangent[0],
        bridge,
        img_query[0],
        img_key[0],
        img_value[0],
    )
    return tuple(grad[None] for grad in grads)


def solution(mesh):
    torus = Mesh(
        mesh.devices.reshape(4, 4, 2, mesh.shape["tensor"]), ("dp_0", "dp_1", "dp_2", "tensor")
    )
    return on_torus(torus)


def on_torus(torus):
    in_specs = (
        P(DP, "tensor", None),
        P(DP, "tensor", None),
        P(),
        P(DP),
        P(DP, "tensor"),
        P(None, "tensor"),
        P(DP, "tensor", None),
        P(DP, "tensor", None),
        P(DP, "tensor", None),
    )
    out_specs = (P(DP, "tensor", None), P(DP, "tensor", None), P(DP, "tensor", None))
    return jax.shard_map(local, mesh=torus, in_specs=in_specs, out_specs=out_specs, check_vma=False)
```

```python
import functools
from typing import NamedTuple, Any

import jax
import jax.numpy as jnp
from jax import lax
from jax.experimental import pallas as pl
from jax.experimental.pallas import tpu as pltpu
from jax.sharding import Mesh
from jax.sharding import PartitionSpec as P

HD = 128
GW = 64
D = 3584
DP = ("dp_0", "dp_1", "dp_2")
SEQ = 2048
VIS = 512
TP = 16
NY, NZ = 4, 4
QB = 512
UB = QB // 4
KC = 256
SCALE = HD**-0.5
DOSES = (3, 3, 7, 11, 15, 15, 45)
LOG2E = 1.4426950408889634
BF = jnp.bfloat16
F32 = jnp.float32

NT = (((1,), (1,)), ((), ()))
NN = (((1,), (0,)), ((), ()))
TN = (((0,), (0,)), ((), ()))


def mm(a, b, dims=NN):
    return lax.dot_general(a, b, dims, preferred_element_type=F32)


class AttnScratch(NamedTuple):
    s_buf: Any
    dp_buf: Any
    perm: Any
    perm_t: Any
    k_t: Any
    dq_t: Any
    dk_acc: Any
    dv_acc: Any


def attn_scratch():
    return [
        pltpu.VMEM((SEQ, QB), F32),
        pltpu.VMEM((SEQ, UB), F32),
        pltpu.VMEM((QB, QB), BF),
        pltpu.VMEM((QB, QB), BF),
        pltpu.VMEM((HD, SEQ), BF),
        pltpu.VMEM((HD, QB), F32),
        pltpu.VMEM((SEQ, HD), F32),
        pltpu.VMEM((SEQ, HD), F32),
    ]


def grouped(rank):
    group, place = rank // UB, rank % UB
    return (place // 32) * HD + (group // 2) * GW + 2 * (place % 32) + group % 2


def attn_tables(env):
    row = lax.broadcasted_iota(jnp.int32, (QB, QB), 0)
    col = lax.broadcasted_iota(jnp.int32, (QB, QB), 1)
    env.perm[...] = (grouped(row) == col).astype(F32).astype(BF)
    env.perm_t[...] = (grouped(col) == row).astype(F32).astype(BF)
    env.dk_acc[...] = jnp.zeros((SEQ, HD), F32)
    env.dv_acc[...] = jnp.zeros((SEQ, HD), F32)


def attn_transpose(env, k_all):
    eye = (
        lax.broadcasted_iota(jnp.int32, (HD, HD), 0)
        == lax.broadcasted_iota(jnp.int32, (HD, HD), 1)
    ).astype(F32).astype(BF)
    env.k_t[...] = mm(eye, k_all[...], NT).astype(BF)


def attn_setup(env, k_all):
    attn_tables(env)
    attn_transpose(env, k_all)


def fold(values, op):
    return op(values.reshape(values.shape[0] // 8, 8, values.shape[1]), axis=0)


def four(values):
    return jnp.concatenate([values] * 4, axis=1)


def attn_block(env, block, q_all, k_all, v_all, hand_all, dq_all):
    q_rows = pl.ds(pl.multiple_of(block * QB, QB), QB)
    q_g = mm(env.perm[...], q_all[q_rows, :]).astype(BF)
    hand = hand_all[pl.ds(pl.multiple_of(block * UB, UB), UB), :]

    def rows(chunk):
        return pl.ds(pl.multiple_of(chunk * KC, KC), KC)

    def scores(chunk, top):
        s = mm(k_all[rows(chunk), :], q_g, NT)
        env.s_buf[rows(chunk), :] = s
        return jnp.maximum(top, fold(s, jnp.max))

    top = lax.fori_loop(0, SEQ // KC, scores, jnp.full((8, QB), -jnp.inf, F32), unroll=2)
    top = jnp.max(top, axis=0, keepdims=True)

    def weights(chunk, carry):
        total, dot_sum = carry
        e = jnp.exp2((env.s_buf[rows(chunk), :] - top) * (SCALE * LOG2E))
        env.s_buf[rows(chunk), :] = e
        dp = mm(v_all[rows(chunk), :], hand, NT)
        env.dp_buf[rows(chunk), :] = dp
        return total + fold(e, jnp.sum), dot_sum + fold(e * four(dp), jnp.sum)

    zeros = jnp.zeros((8, QB), F32)
    total, dot_sum = lax.fori_loop(0, SEQ // KC, weights, (zeros, zeros), unroll=2)
    inv = 1.0 / jnp.sum(total, axis=0, keepdims=True)
    row_dot = jnp.sum(dot_sum, axis=0, keepdims=True) * inv
    env.dq_t[...] = jnp.zeros((HD, QB), F32)

    def grads(chunk, _):
        p = env.s_buf[rows(chunk), :] * inv
        ds = (p * (four(env.dp_buf[rows(chunk), :]) - row_dot)).astype(BF)
        p_sum = (p[:, :UB] + p[:, UB : 2 * UB]) + (p[:, 2 * UB : 3 * UB] + p[:, 3 * UB :])
        env.dk_acc[rows(chunk), :] += mm(ds, q_g)
        env.dv_acc[rows(chunk), :] += mm(p_sum.astype(BF), hand)
        env.dq_t[...] += mm(env.k_t[:, rows(chunk)], ds)
        return 0

    lax.fori_loop(0, SEQ // KC, grads, 0, unroll=2)
    dq_t = (env.dq_t[...] * SCALE).astype(BF)
    dq_all[q_rows, :] = mm(env.perm_t[...], dq_t, NT).astype(BF)


def attn_finish(env, dk_all, dv_all):
    dk_all[...] = (env.dk_acc[...] * SCALE).astype(BF)
    dv_all[...] = env.dv_acc[...].astype(BF)


class Links(NamedTuple):
    x: Any
    z_hi: Any
    core: Any
    tensor: Any
    sizes: tuple


def remote(src, dst, send_sem, recv_sem, device):
    return pltpu.make_async_remote_copy(
        src_ref=src,
        dst_ref=dst,
        send_sem=send_sem,
        recv_sem=recv_sem,
        device_id=device,
        device_id_type=pl.DeviceIdType.MESH,
    )


def kernel(
    sizes,
    rew_ref,
    pos_ref,
    gain_ref,
    hid_hbm,
    cot_hbm,
    bridge_hbm,
    q_hbm,
    k_hbm,
    v_hbm,
    dq_out,
    dk_out,
    dv_out,
    hid,
    cot,
    vg_all,
    bridge_all,
    hand_mine,
    hand_all,
    q_all,
    k_all,
    v_all,
    dq_all,
    dk_all,
    dv_all,
    rew,
    own_sem,
    rew_send,
    rew_recv,
    vg_send,
    vg_recv,
    br_send,
    br_recv,
    hand_send,
    hand_recv,
    q_send,
    q_recv,
    k_send,
    k_recv,
    v_send,
    v_recv,
    dq_send,
    dq_recv,
    dk_send,
    dk_recv,
    dv_send,
    dv_recv,
    *scratch,
):
    env = AttnScratch(*scratch)
    n_x, n_zhi, n_core = sizes
    x, z_hi, core, me = (lax.axis_index(a) for a in (*DP, "tensor"))
    y, z = me // NZ, me % NZ
    axis_of = {"dp_0": (x, n_x), "dp_1": (z_hi, n_zhi), "dp_2": (core, n_core)}

    def turned(name, step):
        place, size = axis_of[name]
        return {name: lax.rem(place + step, size)}

    barrier = pltpu.get_barrier_semaphore()

    def greet(step, _):
        pl.semaphore_signal(
            barrier,
            inc=1,
            device_id={"tensor": lax.rem(me + step, TP)},
            device_id_type=pl.DeviceIdType.MESH,
        )
        return 0

    lax.fori_loop(1, TP, greet, 0)
    partners = TP - 1
    for name, (_, size) in axis_of.items():
        for step in range(1, size):
            pl.semaphore_signal(
                barrier, inc=1, device_id=turned(name, step), device_id_type=pl.DeviceIdType.MESH
            )
            partners += 1

    mine = pl.ds(pl.multiple_of(me * HD, HD), HD)
    my_cols = pl.ds(pl.multiple_of(y * HD, HD), HD)
    local = [
        pltpu.make_async_copy(hid_hbm, hid, own_sem.at[0]),
        pltpu.make_async_copy(cot_hbm, cot, own_sem.at[1]),
        pltpu.make_async_copy(bridge_hbm, bridge_all.at[:, my_cols], own_sem.at[2]),
        pltpu.make_async_copy(k_hbm.at[:, mine], k_all.at[mine, :], own_sem.at[3]),
        pltpu.make_async_copy(v_hbm.at[:, mine], v_all.at[mine, :], own_sem.at[4]),
        pltpu.make_async_copy(q_hbm.at[:, mine], q_all.at[mine, :], own_sem.at[5]),
    ]
    for copy in local:
        copy.start()
    pl.semaphore_wait(barrier, partners)

    def reward_copies(first, name):
        place, size = axis_of[name]
        return [
            remote(
                rew.at[first + place],
                rew.at[first + place],
                rew_send.at[first + step],
                rew_recv.at[first + place],
                turned(name, step),
            )
            for step in range(1, size)
        ]

    def reward_start(first, name, value):
        rew[first + axis_of[name][0]] = value
        for copy in reward_copies(first, name):
            copy.start()

    def reward_sum(first, name):
        place, size = axis_of[name]
        for step in range(1, size):
            other = lax.rem(place + step, size)
            remote(
                rew.at[first + other],
                rew.at[first + other],
                rew_send.at[first + step],
                rew_recv.at[first + other],
                turned(name, step),
            ).wait_recv()
        total = rew[first]
        for slot in range(1, size):
            total = total + rew[first + slot]
        return total

    my_reward = jnp.full((8, HD), rew_ref[0], F32)
    reward_start(0, "dp_2", my_reward)

    half, quarter = D // 2, D // 4
    up, down = {"tensor": lax.rem(y + 1, NY) * NZ + z}, {"tensor": lax.rem(y + NY - 1, NY) * NZ + z}

    def bridge_region(owner, first, count):
        return bridge_all.at[
            pl.ds(pl.multiple_of(first, 16), count),
            pl.ds(pl.multiple_of(owner * HD, HD), HD),
        ]

    def bridge_own(device, slot):
        rows = pl.ds(pl.multiple_of(core * half, 16), half)
        return remote(
            bridge_hbm.at[rows, :],
            bridge_region(y, core * half, half),
            br_send.at[slot],
            br_recv.at[slot],
            device,
        )

    def bridge_copy(owner, first, count, slot, device):
        region = bridge_region(owner, first, count)
        return remote(region, region, br_send.at[slot], br_recv.at[slot], device)

    below, above = lax.rem(y + NY - 1, NY), lax.rem(y + 1, NY)
    across = lax.rem(y + 2, NY)
    bridge_up, bridge_down = bridge_own(up, 0), bridge_own(down, 1)
    bridge_up.start()
    bridge_down.start()

    def peer_at(step):
        d_y, d_z = step // NZ, step % NZ
        return lax.rem(y - d_y + NY, NY) * NZ + lax.rem(z + d_z, NZ)

    def head_send(array, all_ref, sends, recvs, peer):
        cols = pl.ds(pl.multiple_of(peer * HD, HD), HD)
        return remote(
            array.at[:, cols], all_ref.at[mine, :], sends.at[peer], recvs.at[me], {"tensor": peer}
        )

    def head_recv(all_ref, sends, recvs, peer):
        region = all_ref.at[pl.ds(pl.multiple_of(peer * HD, HD), HD), :]
        return remote(region, region, sends.at[peer], recvs.at[peer], {"tensor": peer})

    def to_all(copy_to):
        def one(step, _):
            copy_to(peer_at(step))
            return 0

        lax.fori_loop(1, TP, one, 0)

    heads = (
        (k_hbm, k_all, k_send, k_recv),
        (v_hbm, v_all, v_send, v_recv),
        (q_hbm, q_all, q_send, q_recv),
    )
    moved = [0]

    def move_heads(until):
        while moved[0] < until:
            which, first = divmod(moved[0], TP - 1)
            last = min(TP - 1, first + until - moved[0])

            def one(step, _, refs=heads[which]):
                head_send(*refs, peer_at(step)).start()
                return 0

            lax.fori_loop(first + 1, last + 1, one, 0)
            moved[0] += last - first

    move_heads(DOSES[0])

    local[0].wait()
    local[1].wait()
    local_rows = pos_ref[...] - me * hid.shape[0]
    picked = (
        lax.broadcasted_iota(jnp.int32, (hid.shape[0], local_rows.shape[1]), 0) == local_rows
    )
    picked = picked.astype(F32).astype(BF)
    hidden = mm(picked, hid[...], TN)
    scaled = mm(picked, cot[...], TN) * gain_ref[...].reshape(1, gain_ref.shape[0])
    inv_rms = lax.rsqrt(jnp.mean(hidden * hidden, axis=-1, keepdims=True) + 1e-06)
    mixed = jnp.mean(hidden * scaled, axis=-1, keepdims=True)
    count = local_rows.shape[1]
    vg_all[pl.ds(pl.multiple_of(z * count, count), count), :] = (
        inv_rms * scaled - hidden * (inv_rms * inv_rms * inv_rms * mixed)
    ).astype(BF)

    def vg_copy(owner, slot, device):
        region = vg_all.at[pl.ds(pl.multiple_of(owner * count, count), count), :]
        return remote(region, region, vg_send.at[slot], vg_recv.at[slot], device)

    right = {"tensor": y * NZ + lax.rem(z + 1, NZ)}
    left = {"tensor": y * NZ + lax.rem(z + NZ - 1, NZ)}

    def vg_hop(hop, action):
        @pl.when((z < NZ - 1) & (z >= hop))
        def _():
            action(vg_copy(lax.rem(z - hop + NZ, NZ), hop, right))

        @pl.when((z > 0) & (z + hop < NZ))
        def _():
            action(vg_copy(lax.rem(z + hop, NZ), NZ + hop, left))

    def vg_take(hop):
        @pl.when(z > hop)
        def _():
            vg_copy(lax.rem(z - hop - 1 + NZ, NZ), hop, left).wait_recv()

        @pl.when(z + hop + 1 < NZ)
        def _():
            vg_copy(lax.rem(z + hop + 1, NZ), NZ + hop, right).wait_recv()

    vg_hop(0, lambda copy: copy.start())
    move_heads(DOSES[1])
    core_total = reward_sum(0, "dp_2")
    reward_start(2, "dp_0", core_total)
    attn_tables(env)

    vg_take(0)
    vg_hop(1, lambda copy: copy.start())
    move_heads(DOSES[2])
    x_total = reward_sum(2, "dp_0")
    reward_start(2 + 4, "dp_1", x_total)

    sibling = turned("dp_2", 1)
    bridge_copy(below, core * half, half, 0, down).wait_recv()
    on_up = bridge_copy(below, core * half, quarter, 2, up)
    on_up.start()
    share_below = bridge_copy(below, core * half, half, 4, sibling)
    share_below.start()
    bridge_copy(above, core * half, half, 1, up).wait_recv()
    on_down = bridge_copy(above, core * half + quarter, quarter, 3, down)
    on_down.start()
    share_above = bridge_copy(above, core * half, half, 5, sibling)
    share_above.start()
    move_heads(DOSES[3])
    vg_take(1)
    vg_hop(2, lambda copy: copy.start())
    move_heads(DOSES[4])
    bridge_copy(across, core * half, quarter, 2, down).wait_recv()
    bridge_copy(across, core * half + quarter, quarter, 3, up).wait_recv()
    share_across = bridge_copy(across, core * half, half, 6, sibling)
    share_across.start()
    other = (1 - core) * half
    move_heads(DOSES[5])
    vg_take(2)
    move_heads(DOSES[6])
    z_total = reward_sum(2 + 4, "dp_1")
    weight = rew_ref[0] * (n_x * n_zhi * n_core) / z_total[0:1, :]

    def hand_head(owner):
        cols = pl.ds(pl.multiple_of(owner * HD, HD), HD)
        product = mm(vg_all[...], bridge_all[:, cols])
        return (product * weight).astype(BF)

    my_rows = pl.ds(pl.multiple_of(y * UB, UB), UB)

    def hand_copy(step):
        head = lax.rem(y + step, NY)
        return remote(
            hand_mine.at[step],
            hand_all.at[my_rows, :],
            hand_send.at[step],
            hand_recv.at[y],
            {"tensor": head * NZ + z},
        )

    local[2].wait()
    hand_all[my_rows, :] = hand_head(y)
    for step, slot in ((1, 5), (3, 4), (2, 6)):
        owner = lax.rem(y + step, NY)
        bridge_copy(owner, other, half, slot, sibling).wait_recv()
        hand_mine[step] = hand_head(owner)
        hand_copy(step).start()

    for copy in local[3:]:
        copy.wait()
    to_all(lambda peer: head_recv(k_all, k_send, k_recv, peer).wait_recv())
    attn_transpose(env, k_all)
    to_all(lambda peer: head_recv(v_all, v_send, v_recv, peer).wait_recv())
    for step in range(1, NY):
        src = lax.rem(y + step, NY)
        region = hand_all.at[pl.ds(pl.multiple_of(src * UB, UB), UB), :]
        remote(
            region, region, hand_send.at[step], hand_recv.at[src], {"tensor": src * NZ + z}
        ).wait_recv()

    def token_send(all_ref, out, sends, recvs, peer):
        rows = pl.ds(pl.multiple_of(peer * HD, HD), HD)
        return remote(
            all_ref.at[rows, :], out.at[:, mine], sends.at[peer], recvs.at[me], {"tensor": peer}
        )

    def token_recv(out, sends, recvs, peer):
        region = out.at[:, pl.ds(pl.multiple_of(peer * HD, HD), HD)]
        return remote(region, region, sends.at[peer], recvs.at[peer], {"tensor": peer})

    def token_own(all_ref, out, slot):
        return pltpu.make_async_copy(all_ref.at[mine, :], out.at[:, mine], own_sem.at[slot])

    def attend(step, _):
        block = lax.rem(y + step, NY)

        def take(i, _):
            peer = block * NZ + i

            @pl.when(peer != me)
            def _():
                head_recv(q_all, q_send, q_recv, peer).wait_recv()

            return 0

        lax.fori_loop(0, NZ, take, 0)
        attn_block(env, block, q_all, k_all, v_all, hand_all, dq_all)

        def give(i, _):
            peer = block * NZ + lax.rem(z + i, NZ)

            @pl.when(peer != me)
            def _():
                token_send(dq_all, dq_out, dq_send, dq_recv, peer).start()

            return 0

        lax.fori_loop(0, NZ, give, 0)
        return 0

    lax.fori_loop(0, NY, attend, 0)
    attn_finish(env, dk_all, dv_all)
    to_all(lambda peer: token_send(dk_all, dk_out, dk_send, dk_recv, peer).start())
    to_all(lambda peer: token_send(dv_all, dv_out, dv_send, dv_recv, peer).start())
    own = [
        token_own(dq_all, dq_out, 0),
        token_own(dk_all, dk_out, 1),
        token_own(dv_all, dv_out, 2),
    ]
    for copy in own:
        copy.start()

    for first, name in ((0, "dp_2"), (2, "dp_0"), (2 + 4, "dp_1")):
        for copy in reward_copies(first, name):
            copy.wait_send()
    for copy in (bridge_up, bridge_down, on_up, on_down, share_below, share_above, share_across):
        copy.wait_send()
    for hop in range(NZ - 1):
        vg_hop(hop, lambda copy: copy.wait_send())
    for step in range(1, NY):
        hand_copy(step).wait_send()

    def settle(peer):
        head_send(k_hbm, k_all, k_send, k_recv, peer).wait_send()
        head_send(v_hbm, v_all, v_send, v_recv, peer).wait_send()
        head_send(q_hbm, q_all, q_send, q_recv, peer).wait_send()
        token_send(dq_all, dq_out, dq_send, dq_recv, peer).wait_send()
        token_send(dk_all, dk_out, dk_send, dk_recv, peer).wait_send()
        token_send(dv_all, dv_out, dv_send, dv_recv, peer).wait_send()
        token_recv(dq_out, dq_send, dq_recv, peer).wait_recv()
        token_recv(dk_out, dk_send, dk_recv, peer).wait_recv()
        token_recv(dv_out, dv_send, dv_recv, peer).wait_recv()

    to_all(settle)
    for copy in own:
        copy.wait()


def local(
    rm_hidden, rm_cotangent, rm_gain, rewards, visual_pos, bridge, img_query, img_key, img_value
):
    sizes = tuple(lax.axis_size(a) for a in DP)
    rows, depth = rm_hidden.shape[1:]
    count = visual_pos.shape[1]
    tokens = jax.ShapeDtypeStruct(img_query.shape[1:], BF)
    anywhere = pl.BlockSpec(memory_space=pltpu.HBM)
    in_vmem = pl.BlockSpec(memory_space=pltpu.VMEM)
    group = pltpu.SemaphoreType.DMA((TP,))
    head = pltpu.VMEM((SEQ, HD), BF)
    grads = pl.pallas_call(
        functools.partial(kernel, sizes),
        out_shape=[tokens] * 3,
        in_specs=[pl.BlockSpec(memory_space=pltpu.SMEM), in_vmem, in_vmem] + [anywhere] * 6,
        out_specs=[anywhere] * 3,
        scratch_shapes=[
            pltpu.VMEM((rows, depth), BF),
            pltpu.VMEM((rows, depth), BF),
            pltpu.VMEM((NZ * count, depth), BF),
            pltpu.VMEM((depth, NY * HD), BF),
            pltpu.VMEM((NY, UB, HD), BF),
            pltpu.VMEM((VIS, HD), BF),
            *([head] * 6),
            pltpu.VMEM((2 + 4 + 4, 8, HD), F32),
            pltpu.SemaphoreType.DMA((6,)),
            pltpu.SemaphoreType.DMA((10,)),
            pltpu.SemaphoreType.DMA((10,)),
            pltpu.SemaphoreType.DMA((2 * NZ,)),
            pltpu.SemaphoreType.DMA((2 * NZ,)),
            pltpu.SemaphoreType.DMA((7,)),
            pltpu.SemaphoreType.DMA((7,)),
            pltpu.SemaphoreType.DMA((NY,)),
            pltpu.SemaphoreType.DMA((NY,)),
            *([group] * 12),
            *attn_scratch(),
        ],
        compiler_params=pltpu.CompilerParams(
            collective_id=0, has_side_effects=True, vmem_limit_bytes=63 << 20
        ),
    )(
        rewards,
        visual_pos,
        rm_gain,
        rm_hidden[0],
        rm_cotangent[0],
        bridge,
        img_query[0],
        img_key[0],
        img_value[0],
    )
    return tuple(grad[None] for grad in grads)


def solution(mesh):
    torus = Mesh(
        mesh.devices.reshape(4, 4, 2, mesh.shape["tensor"]), ("dp_0", "dp_1", "dp_2", "tensor")
    )
    return on_torus(torus)


def on_torus(torus):
    in_specs = (
        P(DP, "tensor", None),
        P(DP, "tensor", None),
        P(),
        P(DP),
        P(DP, "tensor"),
        P(None, "tensor"),
        P(DP, "tensor", None),
        P(DP, "tensor", None),
        P(DP, "tensor", None),
    )
    out_specs = (P(DP, "tensor", None), P(DP, "tensor", None), P(DP, "tensor", None))
    return jax.shard_map(local, mesh=torus, in_specs=in_specs, out_specs=out_specs, check_vma=False)
```

```python
import functools
from typing import NamedTuple, Any

import jax
import jax.numpy as jnp
from jax import lax
from jax.experimental import pallas as pl
from jax.experimental.pallas import tpu as pltpu
from jax.sharding import Mesh
from jax.sharding import PartitionSpec as P

HD = 128
GW = 64
D = 3584
DP = ("dp_0", "dp_1", "dp_2")
SEQ = 2048
VIS = 512
TP = 16
NY, NZ = 4, 4
QB = 512
UB = QB // 4
KC = 256
SCALE = HD**-0.5
DOSES = (3, 3, 7, 11, 15, 15, 45)
LOG2E = 1.4426950408889634
BF = jnp.bfloat16
F32 = jnp.float32

NT = (((1,), (1,)), ((), ()))
NN = (((1,), (0,)), ((), ()))
TN = (((0,), (0,)), ((), ()))


def mm(a, b, dims=NN):
    return lax.dot_general(a, b, dims, preferred_element_type=F32)


class AttnScratch(NamedTuple):
    s_buf: Any
    dp_buf: Any
    perm: Any
    perm_t: Any
    k_t: Any
    dq_t: Any
    dk_acc: Any
    dv_acc: Any


def attn_scratch():
    return [
        pltpu.VMEM((SEQ, QB), F32),
        pltpu.VMEM((SEQ, UB), F32),
        pltpu.VMEM((QB, QB), BF),
        pltpu.VMEM((QB, QB), BF),
        pltpu.VMEM((HD, SEQ), BF),
        pltpu.VMEM((HD, QB), F32),
        pltpu.VMEM((SEQ, HD), F32),
        pltpu.VMEM((SEQ, HD), F32),
    ]


def grouped(rank):
    group, place = rank // UB, rank % UB
    return (place // 32) * HD + (group // 2) * GW + 2 * (place % 32) + group % 2


def attn_tables(env):
    row = lax.broadcasted_iota(jnp.int32, (QB, QB), 0)
    col = lax.broadcasted_iota(jnp.int32, (QB, QB), 1)
    env.perm[...] = (grouped(row) == col).astype(F32).astype(BF)
    env.perm_t[...] = (grouped(col) == row).astype(F32).astype(BF)
    env.dk_acc[...] = jnp.zeros((SEQ, HD), F32)
    env.dv_acc[...] = jnp.zeros((SEQ, HD), F32)


def attn_transpose(env, k_all):
    eye = (
        lax.broadcasted_iota(jnp.int32, (HD, HD), 0)
        == lax.broadcasted_iota(jnp.int32, (HD, HD), 1)
    ).astype(F32).astype(BF)
    env.k_t[...] = mm(eye, k_all[...], NT).astype(BF)


def attn_setup(env, k_all):
    attn_tables(env)
    attn_transpose(env, k_all)


def fold(values, op):
    return op(values.reshape(values.shape[0] // 8, 8, values.shape[1]), axis=0)


def four(values):
    return jnp.concatenate([values] * 4, axis=1)


def attn_block(env, block, q_all, k_all, v_all, hand_all):
    q_rows = pl.ds(pl.multiple_of(block * QB, QB), QB)
    q_g = mm(env.perm[...], q_all[q_rows, :]).astype(BF)
    hand = hand_all[pl.ds(pl.multiple_of(block * UB, UB), UB), :]

    def rows(chunk):
        return pl.ds(pl.multiple_of(chunk * KC, KC), KC)

    def scores(chunk, top):
        s = mm(k_all[rows(chunk), :], q_g, NT)
        env.s_buf[rows(chunk), :] = s
        return jnp.maximum(top, fold(s, jnp.max))

    top = lax.fori_loop(0, SEQ // KC, scores, jnp.full((8, QB), -jnp.inf, F32), unroll=2)
    top = jnp.max(top, axis=0, keepdims=True)

    def weights(chunk, carry):
        total, dot_sum = carry
        e = jnp.exp2((env.s_buf[rows(chunk), :] - top) * (SCALE * LOG2E))
        env.s_buf[rows(chunk), :] = e
        dp = mm(v_all[rows(chunk), :], hand, NT)
        env.dp_buf[rows(chunk), :] = dp
        return total + fold(e, jnp.sum), dot_sum + fold(e * four(dp), jnp.sum)

    zeros = jnp.zeros((8, QB), F32)
    total, dot_sum = lax.fori_loop(0, SEQ // KC, weights, (zeros, zeros), unroll=2)
    inv = 1.0 / jnp.sum(total, axis=0, keepdims=True)
    row_dot = jnp.sum(dot_sum, axis=0, keepdims=True) * inv
    env.dq_t[...] = jnp.zeros((HD, QB), F32)

    def grads(chunk, _):
        p = env.s_buf[rows(chunk), :] * inv
        ds = (p * (four(env.dp_buf[rows(chunk), :]) - row_dot)).astype(BF)
        p_sum = (p[:, :UB] + p[:, UB : 2 * UB]) + (p[:, 2 * UB : 3 * UB] + p[:, 3 * UB :])
        env.dk_acc[rows(chunk), :] += mm(ds, q_g)
        env.dv_acc[rows(chunk), :] += mm(p_sum.astype(BF), hand)
        env.dq_t[...] += mm(env.k_t[:, rows(chunk)], ds)
        return 0

    lax.fori_loop(0, SEQ // KC, grads, 0, unroll=2)


def attn_close(env, block, dq_all, weight):
    q_rows = pl.ds(pl.multiple_of(block * QB, QB), QB)
    dq_t = (env.dq_t[...] * four(weight * SCALE)).astype(BF)
    dq_all[q_rows, :] = mm(env.perm_t[...], dq_t, NT).astype(BF)


def attn_finish(env, dk_all, dv_all, weight):
    dk_all[...] = (env.dk_acc[...] * (weight * SCALE)).astype(BF)
    dv_all[...] = (env.dv_acc[...] * weight).astype(BF)


def remote(src, dst, send_sem, recv_sem, device):
    return pltpu.make_async_remote_copy(
        src_ref=src,
        dst_ref=dst,
        send_sem=send_sem,
        recv_sem=recv_sem,
        device_id=device,
        device_id_type=pl.DeviceIdType.MESH,
    )


def kernel(
    sizes,
    rew_ref,
    pos_ref,
    gain_ref,
    hid_hbm,
    cot_hbm,
    bridge_hbm,
    q_hbm,
    k_hbm,
    v_hbm,
    dq_out,
    dk_out,
    dv_out,
    hid,
    cot,
    vg_all,
    bridge_all,
    hand_mine,
    hand_all,
    q_all,
    k_all,
    v_all,
    dq_all,
    dk_all,
    dv_all,
    rew,
    total,
    own_sem,
    group_sem,
    pair_send,
    pair_recv,
    lead_send,
    lead_recv,
    total_send,
    total_recv,
    vg_send,
    vg_recv,
    br_send,
    br_recv,
    hand_send,
    hand_recv,
    q_send,
    q_recv,
    k_send,
    k_recv,
    v_send,
    v_recv,
    dq_send,
    dq_recv,
    dk_send,
    dk_recv,
    dv_send,
    dv_recv,
    *scratch,
):
    env = AttnScratch(*scratch)
    n_x, n_zhi, n_core = sizes
    x, z_hi, core, me = (lax.axis_index(a) for a in (*DP, "tensor"))
    y, z = me // NZ, me % NZ
    axis_of = {"dp_0": (x, n_x), "dp_1": (z_hi, n_zhi), "dp_2": (core, n_core)}

    def turned(name, step):
        place, size = axis_of[name]
        return {name: lax.rem(place + step, size)}

    barrier = pltpu.get_barrier_semaphore()
    first = me == 0
    lead, second = first & (core == 0), first & (core == 1)
    n_leads = n_x * n_zhi
    lead_at = x * n_zhi + z_hi

    def signal(semaphore, device):
        pl.semaphore_signal(
            semaphore, inc=1, device_id=device, device_id_type=pl.DeviceIdType.MESH
        )

    def lead_device(step):
        place = lax.rem(lead_at + step, n_leads)
        return {"dp_0": place // n_zhi, "dp_1": lax.rem(place, n_zhi)}

    sibling = turned("dp_2", 1)

    def greet(step, _):
        peer = lax.rem(me + step, TP)

        @pl.when((peer != 0) | (core == 1))
        def _():
            signal(barrier, {"tensor": peer})

        return 0

    lax.fori_loop(1, TP, greet, 0)

    @pl.when(~second)
    def _():
        signal(barrier, sibling)

    @pl.when(lead)
    def _():
        def greet_lead(step, _):
            signal(barrier, lead_device(step))
            return 0

        lax.fori_loop(1, n_leads, greet_lead, 0)

    mine = pl.ds(pl.multiple_of(me * HD, HD), HD)
    my_cols = pl.ds(pl.multiple_of(y * HD, HD), HD)
    local = [
        pltpu.make_async_copy(hid_hbm, hid, own_sem.at[0]),
        pltpu.make_async_copy(cot_hbm, cot, own_sem.at[1]),
        pltpu.make_async_copy(bridge_hbm, bridge_all.at[:, my_cols], own_sem.at[2]),
        pltpu.make_async_copy(k_hbm.at[:, mine], k_all.at[mine, :], own_sem.at[3]),
        pltpu.make_async_copy(v_hbm.at[:, mine], v_all.at[mine, :], own_sem.at[4]),
        pltpu.make_async_copy(q_hbm.at[:, mine], q_all.at[mine, :], own_sem.at[5]),
    ]
    for copy in local:
        copy.start()
    @pl.when(~lead)
    def _():
        pl.semaphore_wait(barrier, TP)

    @pl.when((~first) & (core == 0))
    def _():
        signal(group_sem, {"tensor": 0})

    @pl.when(second)
    def _():
        signal(group_sem, sibling)

    @pl.when(lead)
    def _():
        pl.semaphore_wait(group_sem, TP)

    my_reward = jnp.full((8, HD), rew_ref[0], F32)

    def pair_copy():
        return remote(rew.at[n_leads], rew.at[n_leads], pair_send, pair_recv, sibling)

    def lead_copy(step):
        slot = rew.at[lead_at]
        return remote(slot, slot, lead_send.at[step], lead_recv.at[lead_at], lead_device(step))

    def total_copy(slot, device):
        return remote(total, total, total_send.at[slot], total_recv, device)

    def each(count, action):
        def one(step, _):
            action(step)
            return 0

        lax.fori_loop(1, count, one, 0)

    def group_copy(step):
        return total_copy(step, {"tensor": lax.rem(me + step, TP)})

    @pl.when(second)
    def _():
        rew[n_leads] = my_reward
        pair_copy().start()

    def rewards_out():
        @pl.when(lead)
        def _():
            pl.semaphore_wait(barrier, n_leads - 1)
            pair_copy().wait_recv()
            rew[lead_at] = my_reward + rew[n_leads]
            each(n_leads, lambda step: lead_copy(step).start())

    def rewards_back():
        @pl.when(lead)
        def _():
            def take_lead(step):
                place = lax.rem(lead_at + step, n_leads)
                slot = rew.at[place]
                remote(
                    slot, slot, lead_send.at[step], lead_recv.at[place], lead_device(step)
                ).wait_recv()

            each(n_leads, take_lead)
            all_pairs = rew[0]
            for place in range(1, n_leads):
                all_pairs = all_pairs + rew[place]
            total[...] = all_pairs
            total_copy(0, sibling).start()
            each(TP, lambda step: group_copy(step).start())

        @pl.when(second)
        def _():
            total_copy(0, sibling).wait_recv()
            each(TP, lambda step: group_copy(step).start())

    half, quarter = D // 2, D // 4
    up, down = {"tensor": lax.rem(y + 1, NY) * NZ + z}, {"tensor": lax.rem(y + NY - 1, NY) * NZ + z}

    def bridge_region(owner, first, count):
        return bridge_all.at[
            pl.ds(pl.multiple_of(first, 16), count),
            pl.ds(pl.multiple_of(owner * HD, HD), HD),
        ]

    def bridge_own(device, slot):
        rows = pl.ds(pl.multiple_of(core * half, 16), half)
        return remote(
            bridge_hbm.at[rows, :],
            bridge_region(y, core * half, half),
            br_send.at[slot],
            br_recv.at[slot],
            device,
        )

    def bridge_copy(owner, first, count, slot, device):
        region = bridge_region(owner, first, count)
        return remote(region, region, br_send.at[slot], br_recv.at[slot], device)

    below, above = lax.rem(y + NY - 1, NY), lax.rem(y + 1, NY)
    across = lax.rem(y + 2, NY)
    bridge_up, bridge_down = bridge_own(up, 0), bridge_own(down, 1)
    bridge_up.start()
    bridge_down.start()

    def peer_at(step):
        d_y, d_z = step // NZ, step % NZ
        return lax.rem(y - d_y + NY, NY) * NZ + lax.rem(z + d_z, NZ)

    def head_send(array, all_ref, sends, recvs, peer):
        cols = pl.ds(pl.multiple_of(peer * HD, HD), HD)
        return remote(
            array.at[:, cols], all_ref.at[mine, :], sends.at[peer], recvs.at[me], {"tensor": peer}
        )

    def head_recv(all_ref, sends, recvs, peer):
        region = all_ref.at[pl.ds(pl.multiple_of(peer * HD, HD), HD), :]
        return remote(region, region, sends.at[peer], recvs.at[peer], {"tensor": peer})

    def to_all(copy_to):
        def one(step, _):
            copy_to(peer_at(step))
            return 0

        lax.fori_loop(1, TP, one, 0)

    heads = (
        (k_hbm, k_all, k_send, k_recv),
        (v_hbm, v_all, v_send, v_recv),
        (q_hbm, q_all, q_send, q_recv),
    )
    moved = [0]

    def move_heads(until):
        while moved[0] < until:
            which, first = divmod(moved[0], TP - 1)
            last = min(TP - 1, first + until - moved[0])

            def one(step, _, refs=heads[which]):
                head_send(*refs, peer_at(step)).start()
                return 0

            lax.fori_loop(first + 1, last + 1, one, 0)
            moved[0] += last - first

    move_heads(DOSES[0])

    local[0].wait()
    local[1].wait()
    local_rows = pos_ref[...] - me * hid.shape[0]
    picked = (
        lax.broadcasted_iota(jnp.int32, (hid.shape[0], local_rows.shape[1]), 0) == local_rows
    )
    picked = picked.astype(F32).astype(BF)
    hidden = mm(picked, hid[...], TN)
    scaled = mm(picked, cot[...], TN) * gain_ref[...].reshape(1, gain_ref.shape[0])
    inv_rms = lax.rsqrt(jnp.mean(hidden * hidden, axis=-1, keepdims=True) + 1e-06)
    mixed = jnp.mean(hidden * scaled, axis=-1, keepdims=True)
    count = local_rows.shape[1]
    vg_all[pl.ds(pl.multiple_of(z * count, count), count), :] = (
        inv_rms * scaled - hidden * (inv_rms * inv_rms * inv_rms * mixed)
    ).astype(BF)

    def vg_copy(owner, slot, device):
        region = vg_all.at[pl.ds(pl.multiple_of(owner * count, count), count), :]
        return remote(region, region, vg_send.at[slot], vg_recv.at[slot], device)

    right = {"tensor": y * NZ + lax.rem(z + 1, NZ)}
    left = {"tensor": y * NZ + lax.rem(z + NZ - 1, NZ)}

    def vg_hop(hop, action):
        @pl.when((z < NZ - 1) & (z >= hop))
        def _():
            action(vg_copy(lax.rem(z - hop + NZ, NZ), hop, right))

        @pl.when((z > 0) & (z + hop < NZ))
        def _():
            action(vg_copy(lax.rem(z + hop, NZ), NZ + hop, left))

    def vg_take(hop):
        @pl.when(z > hop)
        def _():
            vg_copy(lax.rem(z - hop - 1 + NZ, NZ), hop, left).wait_recv()

        @pl.when(z + hop + 1 < NZ)
        def _():
            vg_copy(lax.rem(z + hop + 1, NZ), NZ + hop, right).wait_recv()

    vg_hop(0, lambda copy: copy.start())
    move_heads(DOSES[1])
    attn_tables(env)

    vg_take(0)
    vg_hop(1, lambda copy: copy.start())
    move_heads(DOSES[2])
    rewards_out()

    bridge_copy(below, core * half, half, 0, down).wait_recv()
    on_up = bridge_copy(below, core * half, quarter, 2, up)
    on_up.start()
    share_below = bridge_copy(below, core * half, half, 4, sibling)
    share_below.start()
    bridge_copy(above, core * half, half, 1, up).wait_recv()
    on_down = bridge_copy(above, core * half + quarter, quarter, 3, down)
    on_down.start()
    share_above = bridge_copy(above, core * half, half, 5, sibling)
    share_above.start()
    move_heads(DOSES[3])
    vg_take(1)
    vg_hop(2, lambda copy: copy.start())
    move_heads(DOSES[4])
    bridge_copy(across, core * half, quarter, 2, down).wait_recv()
    bridge_copy(across, core * half + quarter, quarter, 3, up).wait_recv()
    share_across = bridge_copy(across, core * half, half, 6, sibling)
    share_across.start()
    other = (1 - core) * half
    move_heads(DOSES[5])
    vg_take(2)
    move_heads(DOSES[6])

    def hand_head(owner):
        cols = pl.ds(pl.multiple_of(owner * HD, HD), HD)
        product = mm(vg_all[...], bridge_all[:, cols])
        return product.astype(BF)

    my_rows = pl.ds(pl.multiple_of(y * UB, UB), UB)

    def hand_copy(step):
        head = lax.rem(y + step, NY)
        return remote(
            hand_mine.at[step],
            hand_all.at[my_rows, :],
            hand_send.at[step],
            hand_recv.at[y],
            {"tensor": head * NZ + z},
        )

    local[2].wait()
    hand_all[my_rows, :] = hand_head(y)
    for step, slot in ((1, 5), (3, 4), (2, 6)):
        owner = lax.rem(y + step, NY)
        bridge_copy(owner, other, half, slot, sibling).wait_recv()
        hand_mine[step] = hand_head(owner)
        hand_copy(step).start()

    rewards_back()

    for copy in local[3:]:
        copy.wait()
    to_all(lambda peer: head_recv(k_all, k_send, k_recv, peer).wait_recv())
    attn_transpose(env, k_all)
    to_all(lambda peer: head_recv(v_all, v_send, v_recv, peer).wait_recv())
    for step in range(1, NY):
        src = lax.rem(y + step, NY)
        region = hand_all.at[pl.ds(pl.multiple_of(src * UB, UB), UB), :]
        remote(
            region, region, hand_send.at[step], hand_recv.at[src], {"tensor": src * NZ + z}
        ).wait_recv()

    def token_send(all_ref, out, sends, recvs, peer):
        rows = pl.ds(pl.multiple_of(peer * HD, HD), HD)
        return remote(
            all_ref.at[rows, :], out.at[:, mine], sends.at[peer], recvs.at[me], {"tensor": peer}
        )

    def token_recv(out, sends, recvs, peer):
        region = out.at[:, pl.ds(pl.multiple_of(peer * HD, HD), HD)]
        return remote(region, region, sends.at[peer], recvs.at[peer], {"tensor": peer})

    def token_own(all_ref, out, slot):
        return pltpu.make_async_copy(all_ref.at[mine, :], out.at[:, mine], own_sem.at[slot])

    def weight_of():
        return rew_ref[0] * (n_x * n_zhi * n_core) / total[0:1, :]

    def attend(step, _):
        block = lax.rem(y + step, NY)

        def take(i, _):
            peer = block * NZ + i

            @pl.when(peer != me)
            def _():
                head_recv(q_all, q_send, q_recv, peer).wait_recv()

            return 0

        lax.fori_loop(0, NZ, take, 0)
        attn_block(env, block, q_all, k_all, v_all, hand_all)

        @pl.when((step == 0) & ~first)
        def _():
            group_copy(1).wait_recv()

        attn_close(env, block, dq_all, weight_of())

        def give(i, _):
            peer = block * NZ + lax.rem(z + i, NZ)

            @pl.when(peer != me)
            def _():
                token_send(dq_all, dq_out, dq_send, dq_recv, peer).start()

            return 0

        lax.fori_loop(0, NZ, give, 0)
        return 0

    lax.fori_loop(0, NY, attend, 0)
    attn_finish(env, dk_all, dv_all, weight_of())
    to_all(lambda peer: token_send(dk_all, dk_out, dk_send, dk_recv, peer).start())
    to_all(lambda peer: token_send(dv_all, dv_out, dv_send, dv_recv, peer).start())
    own = [
        token_own(dq_all, dq_out, 0),
        token_own(dk_all, dk_out, 1),
        token_own(dv_all, dv_out, 2),
    ]
    for copy in own:
        copy.start()

    @pl.when(second)
    def _():
        pair_copy().wait_send()

    @pl.when(lead)
    def _():
        each(n_leads, lambda step: lead_copy(step).wait_send())
        total_copy(0, sibling).wait_send()

    @pl.when(first)
    def _():
        each(TP, lambda step: group_copy(step).wait_send())

    for copy in (bridge_up, bridge_down, on_up, on_down, share_below, share_above, share_across):
        copy.wait_send()
    for hop in range(NZ - 1):
        vg_hop(hop, lambda copy: copy.wait_send())
    for step in range(1, NY):
        hand_copy(step).wait_send()

    def settle(peer):
        head_send(k_hbm, k_all, k_send, k_recv, peer).wait_send()
        head_send(v_hbm, v_all, v_send, v_recv, peer).wait_send()
        head_send(q_hbm, q_all, q_send, q_recv, peer).wait_send()
        token_send(dq_all, dq_out, dq_send, dq_recv, peer).wait_send()
        token_send(dk_all, dk_out, dk_send, dk_recv, peer).wait_send()
        token_send(dv_all, dv_out, dv_send, dv_recv, peer).wait_send()
        token_recv(dq_out, dq_send, dq_recv, peer).wait_recv()
        token_recv(dk_out, dk_send, dk_recv, peer).wait_recv()
        token_recv(dv_out, dv_send, dv_recv, peer).wait_recv()

    to_all(settle)
    for copy in own:
        copy.wait()


def local(
    rm_hidden, rm_cotangent, rm_gain, rewards, visual_pos, bridge, img_query, img_key, img_value
):
    sizes = tuple(lax.axis_size(a) for a in DP)
    n_leads = sizes[0] * sizes[1]
    rows, depth = rm_hidden.shape[1:]
    count = visual_pos.shape[1]
    tokens = jax.ShapeDtypeStruct(img_query.shape[1:], BF)
    anywhere = pl.BlockSpec(memory_space=pltpu.HBM)
    in_vmem = pl.BlockSpec(memory_space=pltpu.VMEM)
    group = pltpu.SemaphoreType.DMA((TP,))
    head = pltpu.VMEM((SEQ, HD), BF)
    grads = pl.pallas_call(
        functools.partial(kernel, sizes),
        out_shape=[tokens] * 3,
        in_specs=[pl.BlockSpec(memory_space=pltpu.SMEM), in_vmem, in_vmem] + [anywhere] * 6,
        out_specs=[anywhere] * 3,
        scratch_shapes=[
            pltpu.VMEM((rows, depth), BF),
            pltpu.VMEM((rows, depth), BF),
            pltpu.VMEM((NZ * count, depth), BF),
            pltpu.VMEM((depth, NY * HD), BF),
            pltpu.VMEM((NY, UB, HD), BF),
            pltpu.VMEM((VIS, HD), BF),
            *([head] * 6),
            pltpu.VMEM((n_leads + 1, 8, HD), F32),
            pltpu.VMEM((8, HD), F32),
            pltpu.SemaphoreType.DMA((6,)),
            pltpu.SemaphoreType.REGULAR,
            pltpu.SemaphoreType.DMA,
            pltpu.SemaphoreType.DMA,
            pltpu.SemaphoreType.DMA((n_leads,)),
            pltpu.SemaphoreType.DMA((n_leads,)),
            group,
            pltpu.SemaphoreType.DMA,
            pltpu.SemaphoreType.DMA((2 * NZ,)),
            pltpu.SemaphoreType.DMA((2 * NZ,)),
            pltpu.SemaphoreType.DMA((7,)),
            pltpu.SemaphoreType.DMA((7,)),
            pltpu.SemaphoreType.DMA((NY,)),
            pltpu.SemaphoreType.DMA((NY,)),
            *([group] * 12),
            *attn_scratch(),
        ],
        compiler_params=pltpu.CompilerParams(
            collective_id=0, has_side_effects=True, vmem_limit_bytes=63 << 20
        ),
    )(
        rewards,
        visual_pos,
        rm_gain,
        rm_hidden[0],
        rm_cotangent[0],
        bridge,
        img_query[0],
        img_key[0],
        img_value[0],
    )
    return tuple(grad[None] for grad in grads)


def solution(mesh):
    torus = Mesh(
        mesh.devices.reshape(4, 4, 2, mesh.shape["tensor"]), ("dp_0", "dp_1", "dp_2", "tensor")
    )
    return on_torus(torus)


def on_torus(torus):
    in_specs = (
        P(DP, "tensor", None),
        P(DP, "tensor", None),
        P(),
        P(DP),
        P(DP, "tensor"),
        P(None, "tensor"),
        P(DP, "tensor", None),
        P(DP, "tensor", None),
        P(DP, "tensor", None),
    )
    out_specs = (P(DP, "tensor", None), P(DP, "tensor", None), P(DP, "tensor", None))
    return jax.shard_map(local, mesh=torus, in_specs=in_specs, out_specs=out_specs, check_vma=False)
```

```python
import functools
from typing import NamedTuple, Any

import jax
import jax.numpy as jnp
from jax import lax
from jax.experimental import pallas as pl
from jax.experimental.pallas import tpu as pltpu
from jax.sharding import Mesh
from jax.sharding import PartitionSpec as P

HD = 128
GW = 64
D = 3584
DP = ("dp_0", "dp_1", "dp_2")
SEQ = 2048
VIS = 512
TP = 16
NY, NZ = 4, 4
QB = 512
UB = QB // 4
KC = 256
SCALE = HD**-0.5
PARTS = 2
DOSES = (3, 3, 7, 11, 15, 15, 33)
LOG2E = 1.4426950408889634
BF = jnp.bfloat16
F32 = jnp.float32

NT = (((1,), (1,)), ((), ()))
NN = (((1,), (0,)), ((), ()))
TN = (((0,), (0,)), ((), ()))


def mm(a, b, dims=NN):
    return lax.dot_general(a, b, dims, preferred_element_type=F32)


class AttnScratch(NamedTuple):
    s_buf: Any
    dp_buf: Any
    perm: Any
    perm_t: Any
    k_t: Any
    dq_t: Any
    dk_acc: Any
    dv_acc: Any


def attn_scratch():
    return [
        pltpu.VMEM((SEQ, QB), F32),
        pltpu.VMEM((SEQ, UB), F32),
        pltpu.VMEM((QB, QB), BF),
        pltpu.VMEM((QB, QB), BF),
        pltpu.VMEM((HD, SEQ), BF),
        pltpu.VMEM((HD, QB), F32),
        pltpu.VMEM((SEQ, HD), F32),
        pltpu.VMEM((SEQ, HD), F32),
    ]


def grouped(rank):
    group, place = rank // UB, rank % UB
    return (place // 32) * HD + (group // 2) * GW + 2 * (place % 32) + group % 2


def attn_tables(env):
    row = lax.broadcasted_iota(jnp.int32, (QB, QB), 0)
    col = lax.broadcasted_iota(jnp.int32, (QB, QB), 1)
    env.perm[...] = (grouped(row) == col).astype(F32).astype(BF)
    env.perm_t[...] = (grouped(col) == row).astype(F32).astype(BF)
    env.dk_acc[...] = jnp.zeros((SEQ, HD), F32)
    env.dv_acc[...] = jnp.zeros((SEQ, HD), F32)


def attn_transpose(env, k_all):
    eye = (
        lax.broadcasted_iota(jnp.int32, (HD, HD), 0)
        == lax.broadcasted_iota(jnp.int32, (HD, HD), 1)
    ).astype(F32).astype(BF)
    env.k_t[...] = mm(eye, k_all[...], NT).astype(BF)


def attn_setup(env, k_all):
    attn_tables(env)
    attn_transpose(env, k_all)


def fold(values, op):
    return op(values.reshape(values.shape[0] // 8, 8, values.shape[1]), axis=0)


def four(values):
    return jnp.concatenate([values] * 4, axis=1)


def attn_block(env, block, q_all, k_all, v_all, hand_all):
    q_rows = pl.ds(pl.multiple_of(block * QB, QB), QB)
    q_g = mm(env.perm[...], q_all[q_rows, :]).astype(BF)
    hand = hand_all[pl.ds(pl.multiple_of(block * UB, UB), UB), :]

    def rows(chunk):
        return pl.ds(pl.multiple_of(chunk * KC, KC), KC)

    def scores(chunk, top):
        s = mm(k_all[rows(chunk), :], q_g, NT)
        env.s_buf[rows(chunk), :] = s
        return jnp.maximum(top, fold(s, jnp.max))

    top = lax.fori_loop(0, SEQ // KC, scores, jnp.full((8, QB), -jnp.inf, F32), unroll=8)
    top = jnp.max(top, axis=0, keepdims=True)

    def weights(chunk, carry):
        total, dot_sum = carry
        e = jnp.exp2((env.s_buf[rows(chunk), :] - top) * (SCALE * LOG2E))
        env.s_buf[rows(chunk), :] = e
        dp = mm(v_all[rows(chunk), :], hand, NT)
        env.dp_buf[rows(chunk), :] = dp
        return total + fold(e, jnp.sum), dot_sum + fold(e * four(dp), jnp.sum)

    zeros = jnp.zeros((8, QB), F32)
    total, dot_sum = lax.fori_loop(0, SEQ // KC, weights, (zeros, zeros), unroll=8)
    inv = 1.0 / jnp.sum(total, axis=0, keepdims=True)
    row_dot = jnp.sum(dot_sum, axis=0, keepdims=True) * inv
    env.dq_t[...] = jnp.zeros((HD, QB), F32)

    def grads(chunk, _):
        p = env.s_buf[rows(chunk), :] * inv
        ds = (p * (four(env.dp_buf[rows(chunk), :]) - row_dot)).astype(BF)
        p_sum = (p[:, :UB] + p[:, UB : 2 * UB]) + (p[:, 2 * UB : 3 * UB] + p[:, 3 * UB :])
        env.dk_acc[rows(chunk), :] += mm(ds, q_g)
        env.dv_acc[rows(chunk), :] += mm(p_sum.astype(BF), hand)
        env.dq_t[...] += mm(env.k_t[:, rows(chunk)], ds)
        return 0

    lax.fori_loop(0, SEQ // KC, grads, 0, unroll=8)


def attn_close(env, block, dq_all, weight):
    q_rows = pl.ds(pl.multiple_of(block * QB, QB), QB)
    dq_t = (env.dq_t[...] * four(weight * SCALE)).astype(BF)
    dq_all[q_rows, :] = mm(env.perm_t[...], dq_t, NT).astype(BF)


def attn_finish(acc, out, weight):
    out[...] = (acc[...] * weight).astype(BF)


def remote(src, dst, send_sem, recv_sem, device):
    return pltpu.make_async_remote_copy(
        src_ref=src,
        dst_ref=dst,
        send_sem=send_sem,
        recv_sem=recv_sem,
        device_id=device,
        device_id_type=pl.DeviceIdType.MESH,
    )


def kernel(
    sizes,
    rew_ref,
    pos_ref,
    gain_ref,
    hid_hbm,
    cot_hbm,
    bridge_hbm,
    q_hbm,
    k_hbm,
    v_hbm,
    dq_out,
    dk_out,
    dv_out,
    hid,
    cot,
    vg_all,
    bridge_all,
    hand_mine,
    hand_all,
    q_all,
    k_all,
    v_all,
    dq_all,
    dk_all,
    dv_all,
    rew,
    total,
    own_sem,
    group_sem,
    pair_send,
    pair_recv,
    lead_send,
    lead_recv,
    total_send,
    total_recv,
    vg_send,
    vg_recv,
    br_send,
    br_recv,
    hand_send,
    hand_recv,
    q_send,
    q_recv,
    k_send,
    k_recv,
    v_send,
    v_recv,
    dq_send,
    dq_recv,
    dk_send,
    dk_recv,
    dv_send,
    dv_recv,
    *scratch,
):
    env = AttnScratch(*scratch)
    n_x, n_zhi, n_core = sizes
    x, z_hi, core, me = (lax.axis_index(a) for a in (*DP, "tensor"))
    y, z = me // NZ, me % NZ
    axis_of = {"dp_0": (x, n_x), "dp_1": (z_hi, n_zhi), "dp_2": (core, n_core)}

    def turned(name, step):
        place, size = axis_of[name]
        return {name: lax.rem(place + step, size)}

    barrier = pltpu.get_barrier_semaphore()
    first = me == 0
    lead, second = first & (core == 0), first & (core == 1)
    n_leads = n_x * n_zhi
    lead_at = x * n_zhi + z_hi

    def signal(semaphore, device):
        pl.semaphore_signal(
            semaphore, inc=1, device_id=device, device_id_type=pl.DeviceIdType.MESH
        )

    def lead_device(step):
        place = lax.rem(lead_at + step, n_leads)
        return {"dp_0": place // n_zhi, "dp_1": lax.rem(place, n_zhi)}

    sibling = turned("dp_2", 1)

    def greet(step, _):
        peer = lax.rem(me + step, TP)

        @pl.when((peer != 0) | (core == 1))
        def _():
            signal(barrier, {"tensor": peer})

        return 0

    lax.fori_loop(1, TP, greet, 0)

    @pl.when(~second)
    def _():
        signal(barrier, sibling)

    @pl.when(lead)
    def _():
        def greet_lead(step, _):
            signal(barrier, lead_device(step))
            return 0

        lax.fori_loop(1, n_leads, greet_lead, 0)

    mine = pl.ds(pl.multiple_of(me * HD, HD), HD)
    my_cols = pl.ds(pl.multiple_of(y * HD, HD), HD)
    local = [
        pltpu.make_async_copy(hid_hbm, hid, own_sem.at[0]),
        pltpu.make_async_copy(cot_hbm, cot, own_sem.at[1]),
        pltpu.make_async_copy(bridge_hbm, bridge_all.at[:, my_cols], own_sem.at[2]),
        pltpu.make_async_copy(k_hbm.at[:, mine], k_all.at[mine, :], own_sem.at[3]),
        pltpu.make_async_copy(v_hbm.at[:, mine], v_all.at[mine, :], own_sem.at[4]),
        pltpu.make_async_copy(q_hbm.at[:, mine], q_all.at[mine, :], own_sem.at[5]),
    ]
    for copy in local:
        copy.start()
    @pl.when(~lead)
    def _():
        pl.semaphore_wait(barrier, TP)

    @pl.when((~first) & (core == 0))
    def _():
        signal(group_sem, {"tensor": 0})

    @pl.when(second)
    def _():
        signal(group_sem, sibling)

    @pl.when(lead)
    def _():
        pl.semaphore_wait(group_sem, TP)

    my_reward = jnp.full((8, HD), rew_ref[0], F32)

    def pair_copy():
        return remote(rew.at[n_leads], rew.at[n_leads], pair_send, pair_recv, sibling)

    def lead_copy(step):
        slot = rew.at[lead_at]
        return remote(slot, slot, lead_send.at[step], lead_recv.at[lead_at], lead_device(step))

    def total_copy(slot, device):
        return remote(total, total, total_send.at[slot], total_recv, device)

    def each(count, action):
        def one(step, _):
            action(step)
            return 0

        lax.fori_loop(1, count, one, 0)

    def group_copy(step):
        return total_copy(step, {"tensor": lax.rem(me + step, TP)})

    @pl.when(second)
    def _():
        rew[n_leads] = my_reward
        pair_copy().start()

    def rewards_out():
        @pl.when(lead)
        def _():
            pl.semaphore_wait(barrier, n_leads - 1)
            pair_copy().wait_recv()
            rew[lead_at] = my_reward + rew[n_leads]
            each(n_leads, lambda step: lead_copy(step).start())

    def rewards_back():
        @pl.when(lead)
        def _():
            def take_lead(step):
                place = lax.rem(lead_at + step, n_leads)
                slot = rew.at[place]
                remote(
                    slot, slot, lead_send.at[step], lead_recv.at[place], lead_device(step)
                ).wait_recv()

            each(n_leads, take_lead)
            all_pairs = rew[0]
            for place in range(1, n_leads):
                all_pairs = all_pairs + rew[place]
            total[...] = all_pairs
            total_copy(0, sibling).start()
            each(TP, lambda step: group_copy(step).start())

        @pl.when(second)
        def _():
            total_copy(0, sibling).wait_recv()
            each(TP, lambda step: group_copy(step).start())

    half, quarter = D // 2, D // 4
    up, down = {"tensor": lax.rem(y + 1, NY) * NZ + z}, {"tensor": lax.rem(y + NY - 1, NY) * NZ + z}

    def bridge_region(owner, first, count):
        return bridge_all.at[
            pl.ds(pl.multiple_of(first, 16), count),
            pl.ds(pl.multiple_of(owner * HD, HD), HD),
        ]

    def bridge_own(device, slot):
        rows = pl.ds(pl.multiple_of(core * half, 16), half)
        return remote(
            bridge_hbm.at[rows, :],
            bridge_region(y, core * half, half),
            br_send.at[slot],
            br_recv.at[slot],
            device,
        )

    def bridge_copy(owner, first, count, slot, device):
        region = bridge_region(owner, first, count)
        return remote(region, region, br_send.at[slot], br_recv.at[slot], device)

    below, above = lax.rem(y + NY - 1, NY), lax.rem(y + 1, NY)
    across = lax.rem(y + 2, NY)
    bridge_up, bridge_down = bridge_own(up, 0), bridge_own(down, 1)
    bridge_up.start()
    bridge_down.start()

    def peer_at(step):
        d_y, d_z = step // NZ, step % NZ
        return lax.rem(y - d_y + NY, NY) * NZ + lax.rem(z + d_z, NZ)

    def head_send(array, all_ref, sends, recvs, peer):
        cols = pl.ds(pl.multiple_of(peer * HD, HD), HD)
        return remote(
            array.at[:, cols], all_ref.at[mine, :], sends.at[peer], recvs.at[me], {"tensor": peer}
        )

    def head_recv(all_ref, sends, recvs, peer):
        region = all_ref.at[pl.ds(pl.multiple_of(peer * HD, HD), HD), :]
        return remote(region, region, sends.at[peer], recvs.at[peer], {"tensor": peer})

    def to_all(copy_to):
        def one(step, _):
            copy_to(peer_at(step))
            return 0

        lax.fori_loop(1, TP, one, 0)

    heads = (
        (k_hbm, k_all, k_send, k_recv),
        (v_hbm, v_all, v_send, v_recv),
        (q_hbm, q_all, q_send, q_recv),
    )
    moved = [0]

    def move_heads(until):
        while moved[0] < until:
            which, first = divmod(moved[0], TP - 1)
            last = min(TP - 1, first + until - moved[0])

            def one(step, _, refs=heads[which]):
                head_send(*refs, peer_at(step)).start()
                return 0

            lax.fori_loop(first + 1, last + 1, one, 0)
            moved[0] += last - first

    move_heads(DOSES[0])

    local[0].wait()
    local[1].wait()
    local_rows = pos_ref[...] - me * hid.shape[0]
    picked = (
        lax.broadcasted_iota(jnp.int32, (hid.shape[0], local_rows.shape[1]), 0) == local_rows
    )
    picked = picked.astype(F32).astype(BF)
    hidden = mm(picked, hid[...], TN)
    scaled = mm(picked, cot[...], TN) * gain_ref[...].reshape(1, gain_ref.shape[0])
    inv_rms = lax.rsqrt(jnp.mean(hidden * hidden, axis=-1, keepdims=True) + 1e-06)
    mixed = jnp.mean(hidden * scaled, axis=-1, keepdims=True)
    count = local_rows.shape[1]
    vg_all[pl.ds(pl.multiple_of(z * count, count), count), :] = (
        inv_rms * scaled - hidden * (inv_rms * inv_rms * inv_rms * mixed)
    ).astype(BF)

    part = count // PARTS

    def vg_copy(owner, slot, device, at):
        region = vg_all.at[pl.ds(pl.multiple_of(owner * count + at * part, part), part), :]
        slot = at * 2 * NZ + slot
        return remote(region, region, vg_send.at[slot], vg_recv.at[slot], device)

    right = {"tensor": y * NZ + lax.rem(z + 1, NZ)}
    left = {"tensor": y * NZ + lax.rem(z + NZ - 1, NZ)}

    def vg_hop(hop, at, action):
        @pl.when((z < NZ - 1) & (z >= hop))
        def _():
            action(vg_copy(lax.rem(z - hop + NZ, NZ), hop, right, at))

        @pl.when((z > 0) & (z + hop < NZ))
        def _():
            action(vg_copy(lax.rem(z + hop, NZ), NZ + hop, left, at))

    def vg_take(hop, at):
        @pl.when(z > hop)
        def _():
            vg_copy(lax.rem(z - hop - 1 + NZ, NZ), hop, left, at).wait_recv()

        @pl.when(z + hop + 1 < NZ)
        def _():
            vg_copy(lax.rem(z + hop + 1, NZ), NZ + hop, right, at).wait_recv()

    def vg_on(hop):
        for at in range(PARTS):
            vg_take(hop, at)
            if hop + 1 < NZ - 1:
                vg_hop(hop + 1, at, lambda copy: copy.start())

    for at in range(PARTS):
        vg_hop(0, at, lambda copy: copy.start())
    move_heads(DOSES[1])
    attn_tables(env)

    vg_on(0)
    move_heads(DOSES[2])
    rewards_out()

    bridge_copy(below, core * half, half, 0, down).wait_recv()
    on_up = bridge_copy(below, core * half, quarter, 2, up)
    on_up.start()
    share_below = bridge_copy(below, core * half, half, 4, sibling)
    share_below.start()
    bridge_copy(above, core * half, half, 1, up).wait_recv()
    on_down = bridge_copy(above, core * half + quarter, quarter, 3, down)
    on_down.start()
    share_above = bridge_copy(above, core * half, half, 5, sibling)
    share_above.start()
    move_heads(DOSES[3])
    vg_on(1)
    move_heads(DOSES[4])
    bridge_copy(across, core * half, quarter, 2, down).wait_recv()
    bridge_copy(across, core * half + quarter, quarter, 3, up).wait_recv()
    share_across = bridge_copy(across, core * half, half, 6, sibling)
    share_across.start()
    other = (1 - core) * half
    move_heads(DOSES[5])
    vg_on(2)
    move_heads(DOSES[6])

    def hand_head(owner):
        cols = pl.ds(pl.multiple_of(owner * HD, HD), HD)
        product = mm(vg_all[...], bridge_all[:, cols])
        return product.astype(BF)

    my_rows = pl.ds(pl.multiple_of(y * UB, UB), UB)

    def hand_copy(step):
        head = lax.rem(y + step, NY)
        return remote(
            hand_mine.at[step],
            hand_all.at[my_rows, :],
            hand_send.at[step],
            hand_recv.at[y],
            {"tensor": head * NZ + z},
        )

    local[2].wait()
    hand_all[my_rows, :] = hand_head(y)
    for step, slot in ((1, 5), (3, 4), (2, 6)):
        owner = lax.rem(y + step, NY)
        bridge_copy(owner, other, half, slot, sibling).wait_recv()
        hand_mine[step] = hand_head(owner)
        hand_copy(step).start()

    rewards_back()

    for copy in local[3:]:
        copy.wait()
    to_all(lambda peer: head_recv(k_all, k_send, k_recv, peer).wait_recv())
    attn_transpose(env, k_all)
    to_all(lambda peer: head_recv(v_all, v_send, v_recv, peer).wait_recv())
    for step in range(1, NY):
        src = lax.rem(y + step, NY)
        region = hand_all.at[pl.ds(pl.multiple_of(src * UB, UB), UB), :]
        remote(
            region, region, hand_send.at[step], hand_recv.at[src], {"tensor": src * NZ + z}
        ).wait_recv()

    def token_send(all_ref, out, sends, recvs, peer):
        rows = pl.ds(pl.multiple_of(peer * HD, HD), HD)
        return remote(
            all_ref.at[rows, :], out.at[:, mine], sends.at[peer], recvs.at[me], {"tensor": peer}
        )

    def token_recv(out, sends, recvs, peer):
        region = out.at[:, pl.ds(pl.multiple_of(peer * HD, HD), HD)]
        return remote(region, region, sends.at[peer], recvs.at[peer], {"tensor": peer})

    def token_own(all_ref, out, slot):
        return pltpu.make_async_copy(all_ref.at[mine, :], out.at[:, mine], own_sem.at[slot])

    def weight_of():
        return rew_ref[0] * (n_x * n_zhi * n_core) / total[0:1, :]

    def attend(step, _):
        block = lax.rem(y + step, NY)

        @pl.when(step < NY - 1)
        def _():
            def ask(i, _):
                head_send(q_hbm, q_all, q_send, q_recv, peer_at((step + 1) * NZ + i)).start()
                return 0

            lax.fori_loop(0, NZ, ask, 0)

        def take(i, _):
            peer = block * NZ + i

            @pl.when(peer != me)
            def _():
                head_recv(q_all, q_send, q_recv, peer).wait_recv()

            return 0

        lax.fori_loop(0, NZ, take, 0)
        attn_block(env, block, q_all, k_all, v_all, hand_all)

        @pl.when((step == 0) & ~first)
        def _():
            group_copy(1).wait_recv()

        attn_close(env, block, dq_all, weight_of())

        def give(i, _):
            peer = block * NZ + lax.rem(z + i, NZ)

            @pl.when(peer != me)
            def _():
                token_send(dq_all, dq_out, dq_send, dq_recv, peer).start()

            return 0

        lax.fori_loop(0, NZ, give, 0)
        return 0

    lax.fori_loop(0, NY, attend, 0)
    attn_finish(env.dk_acc, dk_all, weight_of() * SCALE)
    to_all(lambda peer: token_send(dk_all, dk_out, dk_send, dk_recv, peer).start())
    attn_finish(env.dv_acc, dv_all, weight_of())
    to_all(lambda peer: token_send(dv_all, dv_out, dv_send, dv_recv, peer).start())
    own = [
        token_own(dq_all, dq_out, 0),
        token_own(dk_all, dk_out, 1),
        token_own(dv_all, dv_out, 2),
    ]
    for copy in own:
        copy.start()

    @pl.when(second)
    def _():
        pair_copy().wait_send()

    @pl.when(lead)
    def _():
        each(n_leads, lambda step: lead_copy(step).wait_send())
        total_copy(0, sibling).wait_send()

    @pl.when(first)
    def _():
        each(TP, lambda step: group_copy(step).wait_send())

    for copy in (bridge_up, bridge_down, on_up, on_down, share_below, share_above, share_across):
        copy.wait_send()
    for hop in range(NZ - 1):
        for at in range(PARTS):
            vg_hop(hop, at, lambda copy: copy.wait_send())
    for step in range(1, NY):
        hand_copy(step).wait_send()

    def settle(peer):
        head_send(k_hbm, k_all, k_send, k_recv, peer).wait_send()
        head_send(v_hbm, v_all, v_send, v_recv, peer).wait_send()
        head_send(q_hbm, q_all, q_send, q_recv, peer).wait_send()
        token_send(dq_all, dq_out, dq_send, dq_recv, peer).wait_send()
        token_send(dk_all, dk_out, dk_send, dk_recv, peer).wait_send()
        token_send(dv_all, dv_out, dv_send, dv_recv, peer).wait_send()
        token_recv(dq_out, dq_send, dq_recv, peer).wait_recv()
        token_recv(dk_out, dk_send, dk_recv, peer).wait_recv()
        token_recv(dv_out, dv_send, dv_recv, peer).wait_recv()

    to_all(settle)
    for copy in own:
        copy.wait()


def local(
    rm_hidden, rm_cotangent, rm_gain, rewards, visual_pos, bridge, img_query, img_key, img_value
):
    sizes = tuple(lax.axis_size(a) for a in DP)
    n_leads = sizes[0] * sizes[1]
    rows, depth = rm_hidden.shape[1:]
    count = visual_pos.shape[1]
    tokens = jax.ShapeDtypeStruct(img_query.shape[1:], BF)
    anywhere = pl.BlockSpec(memory_space=pltpu.HBM)
    in_vmem = pl.BlockSpec(memory_space=pltpu.VMEM)
    group = pltpu.SemaphoreType.DMA((TP,))
    head = pltpu.VMEM((SEQ, HD), BF)
    grads = pl.pallas_call(
        functools.partial(kernel, sizes),
        out_shape=[tokens] * 3,
        in_specs=[pl.BlockSpec(memory_space=pltpu.SMEM), in_vmem, in_vmem] + [anywhere] * 6,
        out_specs=[anywhere] * 3,
        scratch_shapes=[
            pltpu.VMEM((rows, depth), BF),
            pltpu.VMEM((rows, depth), BF),
            pltpu.VMEM((NZ * count, depth), BF),
            pltpu.VMEM((depth, NY * HD), BF),
            pltpu.VMEM((NY, UB, HD), BF),
            pltpu.VMEM((VIS, HD), BF),
            *([head] * 6),
            pltpu.VMEM((n_leads + 1, 8, HD), F32),
            pltpu.VMEM((8, HD), F32),
            pltpu.SemaphoreType.DMA((6,)),
            pltpu.SemaphoreType.REGULAR,
            pltpu.SemaphoreType.DMA,
            pltpu.SemaphoreType.DMA,
            pltpu.SemaphoreType.DMA((n_leads,)),
            pltpu.SemaphoreType.DMA((n_leads,)),
            group,
            pltpu.SemaphoreType.DMA,
            pltpu.SemaphoreType.DMA((2 * NZ * PARTS,)),
            pltpu.SemaphoreType.DMA((2 * NZ * PARTS,)),
            pltpu.SemaphoreType.DMA((7,)),
            pltpu.SemaphoreType.DMA((7,)),
            pltpu.SemaphoreType.DMA((NY,)),
            pltpu.SemaphoreType.DMA((NY,)),
            *([group] * 12),
            *attn_scratch(),
        ],
        compiler_params=pltpu.CompilerParams(
            collective_id=0, has_side_effects=True, vmem_limit_bytes=63 << 20
        ),
    )(
        rewards,
        visual_pos,
        rm_gain,
        rm_hidden[0],
        rm_cotangent[0],
        bridge,
        img_query[0],
        img_key[0],
        img_value[0],
    )
    settled = pl.pallas_call(
        settle_copies,
        out_shape=[tokens] * 3,
        in_specs=[anywhere] * 3,
        out_specs=[anywhere] * 3,
        scratch_shapes=[
            pltpu.VMEM((3, *tokens.shape), BF),
            pltpu.SemaphoreType.DMA((3, 4)),
            pltpu.SemaphoreType.DMA((3, 4)),
        ],
    )(*grads)
    return tuple(grad[None] for grad in settled)


def settle_copies(*refs):
    held, came, went = refs[6:]
    part = held.shape[1] // 4
    pieces = [(i, k, pl.ds(k * part, part)) for i in range(3) for k in range(4)]
    into = [
        pltpu.make_async_copy(refs[i].at[rows, :], held.at[i, rows, :], came.at[i, k])
        for i, k, rows in pieces
    ]
    out = [
        pltpu.make_async_copy(held.at[i, rows, :], refs[i + 3].at[rows, :], went.at[i, k])
        for i, k, rows in pieces
    ]
    for copy in into:
        copy.start()
    for arrived, copy in zip(into, out):
        arrived.wait()
        copy.start()
    for copy in out:
        copy.wait()


def solution(mesh):
    torus = Mesh(
        mesh.devices.reshape(4, 4, 2, mesh.shape["tensor"]), ("dp_0", "dp_1", "dp_2", "tensor")
    )
    return on_torus(torus)


def on_torus(torus):
    in_specs = (
        P(DP, "tensor", None),
        P(DP, "tensor", None),
        P(),
        P(DP),
        P(DP, "tensor"),
        P(None, "tensor"),
        P(DP, "tensor", None),
        P(DP, "tensor", None),
        P(DP, "tensor", None),
    )
    out_specs = (P(DP, "tensor", None), P(DP, "tensor", None), P(DP, "tensor", None))
    return jax.shard_map(local, mesh=torus, in_specs=in_specs, out_specs=out_specs, check_vma=False)
```

```python
import functools
from typing import NamedTuple, Any

import jax
import jax.numpy as jnp
from jax import lax
from jax.experimental import pallas as pl
from jax.experimental.pallas import tpu as pltpu
from jax.sharding import Mesh
from jax.sharding import PartitionSpec as P

HD = 128
GW = 64
D = 3584
DP = ("dp_0", "dp_1", "dp_2")
SEQ = 2048
VIS = 512
TP = 16
NY, NZ = 4, 4
QB = 512
UB = QB // 4
KC = 256
SCALE = HD**-0.5
PARTS = 2
DOSES = (3, 3, 7, 11, 15, 15, 33)
LOG2E = 1.4426950408889634
BF = jnp.bfloat16
F32 = jnp.float32

NT = (((1,), (1,)), ((), ()))
NN = (((1,), (0,)), ((), ()))
TN = (((0,), (0,)), ((), ()))


def mm(a, b, dims=NN):
    return lax.dot_general(a, b, dims, preferred_element_type=F32)


class AttnScratch(NamedTuple):
    s_buf: Any
    dp_buf: Any
    perm: Any
    perm_t: Any
    k_t: Any
    dq_t: Any
    dk_acc: Any
    dv_acc: Any


def attn_scratch():
    return [
        pltpu.VMEM((SEQ, QB), F32),
        pltpu.VMEM((SEQ, UB), F32),
        pltpu.VMEM((QB, QB), BF),
        pltpu.VMEM((QB, QB), BF),
        pltpu.VMEM((HD, SEQ), BF),
        pltpu.VMEM((HD, QB), F32),
        pltpu.VMEM((SEQ, HD), F32),
        pltpu.VMEM((SEQ, HD), F32),
    ]


def grouped(rank):
    group, place = rank // UB, rank % UB
    return (place // 32) * HD + (group // 2) * GW + 2 * (place % 32) + group % 2


def attn_tables(env):
    row = lax.broadcasted_iota(jnp.int32, (QB, QB), 0)
    col = lax.broadcasted_iota(jnp.int32, (QB, QB), 1)
    env.perm[...] = (grouped(row) == col).astype(F32).astype(BF)
    env.perm_t[...] = (grouped(col) == row).astype(F32).astype(BF)
    env.dk_acc[...] = jnp.zeros((SEQ, HD), F32)
    env.dv_acc[...] = jnp.zeros((SEQ, HD), F32)


def attn_transpose(env, k_all):
    eye = (
        lax.broadcasted_iota(jnp.int32, (HD, HD), 0)
        == lax.broadcasted_iota(jnp.int32, (HD, HD), 1)
    ).astype(F32).astype(BF)
    env.k_t[...] = mm(eye, k_all[...], NT).astype(BF)


def attn_setup(env, k_all):
    attn_tables(env)
    attn_transpose(env, k_all)


def fold(values, op):
    return op(values.reshape(values.shape[0] // 8, 8, values.shape[1]), axis=0)


def four(values):
    return jnp.concatenate([values] * 4, axis=1)


def attn_block(env, block, q_all, k_all, v_all, hand_all):
    q_rows = pl.ds(pl.multiple_of(block * QB, QB), QB)
    q_g = mm(env.perm[...], q_all[q_rows, :]).astype(BF)
    hand = hand_all[pl.ds(pl.multiple_of(block * UB, UB), UB), :]

    def rows(chunk):
        return pl.ds(pl.multiple_of(chunk * KC, KC), KC)

    def scores(chunk, top):
        s = mm(k_all[rows(chunk), :], q_g, NT)
        env.s_buf[rows(chunk), :] = s
        return jnp.maximum(top, fold(s, jnp.max))

    top = lax.fori_loop(0, SEQ // KC, scores, jnp.full((8, QB), -jnp.inf, F32), unroll=8)
    top = jnp.max(top, axis=0, keepdims=True)

    def weights(chunk, carry):
        total, dot_sum = carry
        e = jnp.exp2((env.s_buf[rows(chunk), :] - top) * (SCALE * LOG2E))
        env.s_buf[rows(chunk), :] = e
        dp = mm(v_all[rows(chunk), :], hand, NT)
        env.dp_buf[rows(chunk), :] = dp
        return total + fold(e, jnp.sum), dot_sum + fold(e * four(dp), jnp.sum)

    zeros = jnp.zeros((8, QB), F32)
    total, dot_sum = lax.fori_loop(0, SEQ // KC, weights, (zeros, zeros), unroll=8)
    inv = 1.0 / jnp.sum(total, axis=0, keepdims=True)
    row_dot = jnp.sum(dot_sum, axis=0, keepdims=True) * inv
    env.dq_t[...] = jnp.zeros((HD, QB), F32)

    def grads(chunk, _):
        p = env.s_buf[rows(chunk), :] * inv
        ds = (p * (four(env.dp_buf[rows(chunk), :]) - row_dot)).astype(BF)
        p_sum = (p[:, :UB] + p[:, UB : 2 * UB]) + (p[:, 2 * UB : 3 * UB] + p[:, 3 * UB :])
        env.dk_acc[rows(chunk), :] += mm(ds, q_g)
        env.dv_acc[rows(chunk), :] += mm(p_sum.astype(BF), hand)
        env.dq_t[...] += mm(env.k_t[:, rows(chunk)], ds)
        return 0

    lax.fori_loop(0, SEQ // KC, grads, 0, unroll=8)


def attn_close(env, block, dq_all, weight):
    q_rows = pl.ds(pl.multiple_of(block * QB, QB), QB)
    dq_t = (env.dq_t[...] * four(weight * SCALE)).astype(BF)
    dq_all[q_rows, :] = mm(env.perm_t[...], dq_t, NT).astype(BF)


def attn_finish(acc, out, weight):
    out[...] = (acc[...] * weight).astype(BF)


def remote(src, dst, send_sem, recv_sem, device):
    return pltpu.make_async_remote_copy(
        src_ref=src,
        dst_ref=dst,
        send_sem=send_sem,
        recv_sem=recv_sem,
        device_id=device,
        device_id_type=pl.DeviceIdType.MESH,
    )


def kernel(
    sizes,
    rew_ref,
    pos_ref,
    gain_ref,
    hid_hbm,
    cot_hbm,
    bridge_hbm,
    q_hbm,
    k_hbm,
    v_hbm,
    dq_out,
    dk_out,
    dv_out,
    hid,
    cot,
    vg_all,
    bridge_all,
    hand_mine,
    hand_all,
    q_all,
    k_all,
    v_all,
    dq_all,
    dk_all,
    dv_all,
    rew,
    total,
    own_sem,
    group_sem,
    pair_send,
    pair_recv,
    lead_send,
    lead_recv,
    total_send,
    total_recv,
    vg_send,
    vg_recv,
    br_send,
    br_recv,
    hand_send,
    hand_recv,
    q_send,
    q_recv,
    k_send,
    k_recv,
    v_send,
    v_recv,
    dq_send,
    dq_recv,
    dk_send,
    dk_recv,
    dv_send,
    dv_recv,
    *scratch,
):
    env = AttnScratch(*scratch)
    n_x, n_zhi, n_core = sizes
    x, z_hi, core, me = (lax.axis_index(a) for a in (*DP, "tensor"))
    y, z = me // NZ, me % NZ
    axis_of = {"dp_0": (x, n_x), "dp_1": (z_hi, n_zhi), "dp_2": (core, n_core)}

    def turned(name, step):
        place, size = axis_of[name]
        return {name: lax.rem(place + step, size)}

    barrier = pltpu.get_barrier_semaphore()
    first = me == 0
    lead, second = first & (core == 0), first & (core == 1)
    n_leads = n_x * n_zhi
    lead_at = x * n_zhi + z_hi

    def signal(semaphore, device):
        pl.semaphore_signal(
            semaphore, inc=1, device_id=device, device_id_type=pl.DeviceIdType.MESH
        )

    def lead_device(step):
        place = lax.rem(lead_at + step, n_leads)
        return {"dp_0": place // n_zhi, "dp_1": lax.rem(place, n_zhi)}

    sibling = turned("dp_2", 1)

    def greet(step, _):
        peer = lax.rem(me + step, TP)

        @pl.when((peer != 0) | (core == 1))
        def _():
            signal(barrier, {"tensor": peer})

        return 0

    lax.fori_loop(1, TP, greet, 0)

    @pl.when(~second)
    def _():
        signal(barrier, sibling)

    @pl.when(lead)
    def _():
        def greet_lead(step, _):
            signal(barrier, lead_device(step))
            return 0

        lax.fori_loop(1, n_leads, greet_lead, 0)

    mine = pl.ds(pl.multiple_of(me * HD, HD), HD)
    my_cols = pl.ds(pl.multiple_of(y * HD, HD), HD)
    local = [
        pltpu.make_async_copy(hid_hbm, hid, own_sem.at[0]),
        pltpu.make_async_copy(cot_hbm, cot, own_sem.at[1]),
        pltpu.make_async_copy(bridge_hbm, bridge_all.at[:, my_cols], own_sem.at[2]),
        pltpu.make_async_copy(k_hbm.at[:, mine], k_all.at[mine, :], own_sem.at[3]),
        pltpu.make_async_copy(v_hbm.at[:, mine], v_all.at[mine, :], own_sem.at[4]),
        pltpu.make_async_copy(q_hbm.at[:, mine], q_all.at[mine, :], own_sem.at[5]),
    ]
    for copy in local:
        copy.start()
    @pl.when(~lead)
    def _():
        pl.semaphore_wait(barrier, TP)

    @pl.when((~first) & (core == 0))
    def _():
        signal(group_sem, {"tensor": 0})

    @pl.when(second)
    def _():
        signal(group_sem, sibling)

    @pl.when(lead)
    def _():
        pl.semaphore_wait(group_sem, TP)

    my_reward = jnp.full((8, HD), rew_ref[0], F32)

    def pair_copy():
        return remote(rew.at[n_leads], rew.at[n_leads], pair_send, pair_recv, sibling)

    def lead_copy(step):
        slot = rew.at[lead_at]
        return remote(slot, slot, lead_send.at[step], lead_recv.at[lead_at], lead_device(step))

    def total_copy(slot, device):
        return remote(total, total, total_send.at[slot], total_recv, device)

    def each(count, action):
        def one(step, _):
            action(step)
            return 0

        lax.fori_loop(1, count, one, 0)

    def group_copy(step):
        return total_copy(step, {"tensor": lax.rem(me + step, TP)})

    @pl.when(second)
    def _():
        rew[n_leads] = my_reward
        pair_copy().start()

    def rewards_out():
        @pl.when(lead)
        def _():
            pl.semaphore_wait(barrier, n_leads - 1)
            pair_copy().wait_recv()
            rew[lead_at] = my_reward + rew[n_leads]
            each(n_leads, lambda step: lead_copy(step).start())

    def rewards_back():
        @pl.when(lead)
        def _():
            def take_lead(step):
                place = lax.rem(lead_at + step, n_leads)
                slot = rew.at[place]
                remote(
                    slot, slot, lead_send.at[step], lead_recv.at[place], lead_device(step)
                ).wait_recv()

            each(n_leads, take_lead)
            all_pairs = rew[0]
            for place in range(1, n_leads):
                all_pairs = all_pairs + rew[place]
            total[...] = all_pairs
            total_copy(0, sibling).start()
            each(TP, lambda step: group_copy(step).start())

        @pl.when(second)
        def _():
            total_copy(0, sibling).wait_recv()
            each(TP, lambda step: group_copy(step).start())

    half, quarter = D // 2, D // 4
    up, down = {"tensor": lax.rem(y + 1, NY) * NZ + z}, {"tensor": lax.rem(y + NY - 1, NY) * NZ + z}

    def bridge_region(owner, first, count):
        return bridge_all.at[
            pl.ds(pl.multiple_of(first, 16), count),
            pl.ds(pl.multiple_of(owner * HD, HD), HD),
        ]

    def bridge_own(device, slot):
        rows = pl.ds(pl.multiple_of(core * half, 16), half)
        return remote(
            bridge_hbm.at[rows, :],
            bridge_region(y, core * half, half),
            br_send.at[slot],
            br_recv.at[slot],
            device,
        )

    def bridge_copy(owner, first, count, slot, device):
        region = bridge_region(owner, first, count)
        return remote(region, region, br_send.at[slot], br_recv.at[slot], device)

    below, above = lax.rem(y + NY - 1, NY), lax.rem(y + 1, NY)
    across = lax.rem(y + 2, NY)
    bridge_up, bridge_down = bridge_own(up, 0), bridge_own(down, 1)
    bridge_up.start()
    bridge_down.start()

    def peer_at(step):
        d_y, d_z = step // NZ, step % NZ
        return lax.rem(y - d_y + NY, NY) * NZ + lax.rem(z + d_z, NZ)

    def head_send(array, all_ref, sends, recvs, peer):
        cols = pl.ds(pl.multiple_of(peer * HD, HD), HD)
        return remote(
            array.at[:, cols], all_ref.at[mine, :], sends.at[peer], recvs.at[me], {"tensor": peer}
        )

    def head_recv(all_ref, sends, recvs, peer):
        region = all_ref.at[pl.ds(pl.multiple_of(peer * HD, HD), HD), :]
        return remote(region, region, sends.at[peer], recvs.at[peer], {"tensor": peer})

    def to_all(copy_to):
        def one(step, _):
            copy_to(peer_at(lax.rem(step, NY) * NZ + step // NY))
            return 0

        lax.fori_loop(1, TP, one, 0)

    heads = (
        (k_hbm, k_all, k_send, k_recv),
        (v_hbm, v_all, v_send, v_recv),
        (q_hbm, q_all, q_send, q_recv),
    )
    moved = [0]

    def move_heads(until):
        while moved[0] < until:
            which, first = divmod(moved[0], TP - 1)
            last = min(TP - 1, first + until - moved[0])

            def one(step, _, refs=heads[which]):
                head_send(*refs, peer_at(step)).start()
                return 0

            lax.fori_loop(first + 1, last + 1, one, 0)
            moved[0] += last - first

    move_heads(DOSES[0])

    local[0].wait()
    local[1].wait()
    local_rows = pos_ref[...] - me * hid.shape[0]
    picked = (
        lax.broadcasted_iota(jnp.int32, (hid.shape[0], local_rows.shape[1]), 0) == local_rows
    )
    picked = picked.astype(F32).astype(BF)
    hidden = mm(picked, hid[...], TN)
    scaled = mm(picked, cot[...], TN) * gain_ref[...].reshape(1, gain_ref.shape[0])
    inv_rms = lax.rsqrt(jnp.mean(hidden * hidden, axis=-1, keepdims=True) + 1e-06)
    mixed = jnp.mean(hidden * scaled, axis=-1, keepdims=True)
    count = local_rows.shape[1]
    vg_all[pl.ds(pl.multiple_of(z * count, count), count), :] = (
        inv_rms * scaled - hidden * (inv_rms * inv_rms * inv_rms * mixed)
    ).astype(BF)

    part = count // PARTS

    def vg_copy(owner, slot, device, at):
        region = vg_all.at[pl.ds(pl.multiple_of(owner * count + at * part, part), part), :]
        slot = at * 2 * NZ + slot
        return remote(region, region, vg_send.at[slot], vg_recv.at[slot], device)

    right = {"tensor": y * NZ + lax.rem(z + 1, NZ)}
    left = {"tensor": y * NZ + lax.rem(z + NZ - 1, NZ)}

    def vg_hop(hop, at, action):
        @pl.when((z < NZ - 1) & (z >= hop))
        def _():
            action(vg_copy(lax.rem(z - hop + NZ, NZ), hop, right, at))

        @pl.when((z > 0) & (z + hop < NZ))
        def _():
            action(vg_copy(lax.rem(z + hop, NZ), NZ + hop, left, at))

    def vg_take(hop, at):
        @pl.when(z > hop)
        def _():
            vg_copy(lax.rem(z - hop - 1 + NZ, NZ), hop, left, at).wait_recv()

        @pl.when(z + hop + 1 < NZ)
        def _():
            vg_copy(lax.rem(z + hop + 1, NZ), NZ + hop, right, at).wait_recv()

    def vg_on(hop):
        for at in range(PARTS):
            vg_take(hop, at)
            if hop + 1 < NZ - 1:
                vg_hop(hop + 1, at, lambda copy: copy.start())

    for at in range(PARTS):
        vg_hop(0, at, lambda copy: copy.start())
    move_heads(DOSES[1])
    attn_tables(env)

    rewards_out()
    vg_on(0)
    move_heads(DOSES[2])
    bridge_copy(below, core * half, half, 0, down).wait_recv()
    on_up = bridge_copy(below, core * half, quarter, 2, up)
    on_up.start()
    share_below = bridge_copy(below, core * half, half, 4, sibling)
    share_below.start()
    bridge_copy(above, core * half, half, 1, up).wait_recv()
    on_down = bridge_copy(above, core * half + quarter, quarter, 3, down)
    on_down.start()
    share_above = bridge_copy(above, core * half, half, 5, sibling)
    share_above.start()
    move_heads(DOSES[3])
    vg_on(1)
    move_heads(DOSES[4])
    bridge_copy(across, core * half, quarter, 2, down).wait_recv()
    bridge_copy(across, core * half + quarter, quarter, 3, up).wait_recv()
    share_across = bridge_copy(across, core * half, half, 6, sibling)
    share_across.start()
    other = (1 - core) * half
    move_heads(DOSES[5])
    vg_on(2)
    move_heads(DOSES[6])

    def hand_head(owner):
        cols = pl.ds(pl.multiple_of(owner * HD, HD), HD)
        product = mm(vg_all[...], bridge_all[:, cols])
        return product.astype(BF)

    my_rows = pl.ds(pl.multiple_of(y * UB, UB), UB)

    def hand_copy(step):
        head = lax.rem(y + step, NY)
        return remote(
            hand_mine.at[step],
            hand_all.at[my_rows, :],
            hand_send.at[step],
            hand_recv.at[y],
            {"tensor": head * NZ + z},
        )

    local[2].wait()
    hand_all[my_rows, :] = hand_head(y)
    for step, slot in ((1, 5), (3, 4), (2, 6)):
        owner = lax.rem(y + step, NY)
        bridge_copy(owner, other, half, slot, sibling).wait_recv()
        hand_mine[step] = hand_head(owner)
        hand_copy(step).start()

    rewards_back()

    for copy in local[3:]:
        copy.wait()
    to_all(lambda peer: head_recv(k_all, k_send, k_recv, peer).wait_recv())
    attn_transpose(env, k_all)
    to_all(lambda peer: head_recv(v_all, v_send, v_recv, peer).wait_recv())
    for step in range(1, NY):
        src = lax.rem(y + step, NY)
        region = hand_all.at[pl.ds(pl.multiple_of(src * UB, UB), UB), :]
        remote(
            region, region, hand_send.at[step], hand_recv.at[src], {"tensor": src * NZ + z}
        ).wait_recv()

    def token_send(all_ref, out, sends, recvs, peer):
        rows = pl.ds(pl.multiple_of(peer * HD, HD), HD)
        return remote(
            all_ref.at[rows, :], out.at[:, mine], sends.at[peer], recvs.at[me], {"tensor": peer}
        )

    def token_recv(out, sends, recvs, peer):
        region = out.at[:, pl.ds(pl.multiple_of(peer * HD, HD), HD)]
        return remote(region, region, sends.at[peer], recvs.at[peer], {"tensor": peer})

    def token_own(all_ref, out, slot):
        return pltpu.make_async_copy(all_ref.at[mine, :], out.at[:, mine], own_sem.at[slot])

    def weight_of():
        return rew_ref[0] * (n_x * n_zhi * n_core) / total[0:1, :]

    def attend(step, _):
        block = lax.rem(y + step, NY)

        @pl.when(step < NY - 1)
        def _():
            def ask(i, _):
                head_send(q_hbm, q_all, q_send, q_recv, peer_at((step + 1) * NZ + i)).start()
                return 0

            lax.fori_loop(0, NZ, ask, 0)

        def take(i, _):
            peer = block * NZ + i

            @pl.when(peer != me)
            def _():
                head_recv(q_all, q_send, q_recv, peer).wait_recv()

            return 0

        lax.fori_loop(0, NZ, take, 0)
        attn_block(env, block, q_all, k_all, v_all, hand_all)

        @pl.when((step == 0) & ~first)
        def _():
            group_copy(1).wait_recv()

        attn_close(env, block, dq_all, weight_of())

        def give(i, _):
            peer = block * NZ + lax.rem(z + i, NZ)

            @pl.when(peer != me)
            def _():
                token_send(dq_all, dq_out, dq_send, dq_recv, peer).start()

            return 0

        lax.fori_loop(0, NZ, give, 0)
        return 0

    lax.fori_loop(0, NY, attend, 0)
    attn_finish(env.dk_acc, dk_all, weight_of() * SCALE)
    to_all(lambda peer: token_send(dk_all, dk_out, dk_send, dk_recv, peer).start())
    attn_finish(env.dv_acc, dv_all, weight_of())
    to_all(lambda peer: token_send(dv_all, dv_out, dv_send, dv_recv, peer).start())
    own = [
        token_own(dq_all, dq_out, 0),
        token_own(dk_all, dk_out, 1),
        token_own(dv_all, dv_out, 2),
    ]
    for copy in own:
        copy.start()

    @pl.when(second)
    def _():
        pair_copy().wait_send()

    @pl.when(lead)
    def _():
        each(n_leads, lambda step: lead_copy(step).wait_send())
        total_copy(0, sibling).wait_send()

    @pl.when(first)
    def _():
        each(TP, lambda step: group_copy(step).wait_send())

    for copy in (bridge_up, bridge_down, on_up, on_down, share_below, share_above, share_across):
        copy.wait_send()
    for hop in range(NZ - 1):
        for at in range(PARTS):
            vg_hop(hop, at, lambda copy: copy.wait_send())
    for step in range(1, NY):
        hand_copy(step).wait_send()

    def settle(peer):
        head_send(k_hbm, k_all, k_send, k_recv, peer).wait_send()
        head_send(v_hbm, v_all, v_send, v_recv, peer).wait_send()
        head_send(q_hbm, q_all, q_send, q_recv, peer).wait_send()
        token_send(dq_all, dq_out, dq_send, dq_recv, peer).wait_send()
        token_send(dk_all, dk_out, dk_send, dk_recv, peer).wait_send()
        token_send(dv_all, dv_out, dv_send, dv_recv, peer).wait_send()
        token_recv(dq_out, dq_send, dq_recv, peer).wait_recv()
        token_recv(dk_out, dk_send, dk_recv, peer).wait_recv()
        token_recv(dv_out, dv_send, dv_recv, peer).wait_recv()

    to_all(settle)
    for copy in own:
        copy.wait()


def local(
    rm_hidden, rm_cotangent, rm_gain, rewards, visual_pos, bridge, img_query, img_key, img_value
):
    sizes = tuple(lax.axis_size(a) for a in DP)
    n_leads = sizes[0] * sizes[1]
    rows, depth = rm_hidden.shape[1:]
    count = visual_pos.shape[1]
    tokens = jax.ShapeDtypeStruct(img_query.shape[1:], BF)
    anywhere = pl.BlockSpec(memory_space=pltpu.HBM)
    in_vmem = pl.BlockSpec(memory_space=pltpu.VMEM)
    group = pltpu.SemaphoreType.DMA((TP,))
    head = pltpu.VMEM((SEQ, HD), BF)
    grads = pl.pallas_call(
        functools.partial(kernel, sizes),
        out_shape=[tokens] * 3,
        in_specs=[pl.BlockSpec(memory_space=pltpu.SMEM), in_vmem, in_vmem] + [anywhere] * 6,
        out_specs=[anywhere] * 3,
        scratch_shapes=[
            pltpu.VMEM((rows, depth), BF),
            pltpu.VMEM((rows, depth), BF),
            pltpu.VMEM((NZ * count, depth), BF),
            pltpu.VMEM((depth, NY * HD), BF),
            pltpu.VMEM((NY, UB, HD), BF),
            pltpu.VMEM((VIS, HD), BF),
            *([head] * 6),
            pltpu.VMEM((n_leads + 1, 8, HD), F32),
            pltpu.VMEM((8, HD), F32),
            pltpu.SemaphoreType.DMA((6,)),
            pltpu.SemaphoreType.REGULAR,
            pltpu.SemaphoreType.DMA,
            pltpu.SemaphoreType.DMA,
            pltpu.SemaphoreType.DMA((n_leads,)),
            pltpu.SemaphoreType.DMA((n_leads,)),
            group,
            pltpu.SemaphoreType.DMA,
            pltpu.SemaphoreType.DMA((2 * NZ * PARTS,)),
            pltpu.SemaphoreType.DMA((2 * NZ * PARTS,)),
            pltpu.SemaphoreType.DMA((7,)),
            pltpu.SemaphoreType.DMA((7,)),
            pltpu.SemaphoreType.DMA((NY,)),
            pltpu.SemaphoreType.DMA((NY,)),
            *([group] * 12),
            *attn_scratch(),
        ],
        compiler_params=pltpu.CompilerParams(
            collective_id=0, has_side_effects=True, vmem_limit_bytes=63 << 20
        ),
    )(
        rewards,
        visual_pos,
        rm_gain,
        rm_hidden[0],
        rm_cotangent[0],
        bridge,
        img_query[0],
        img_key[0],
        img_value[0],
    )
    settled = pl.pallas_call(
        settle_copies,
        out_shape=[tokens] * 3,
        in_specs=[anywhere] * 3,
        out_specs=[anywhere] * 3,
        scratch_shapes=[
            pltpu.VMEM((3, *tokens.shape), BF),
            pltpu.SemaphoreType.DMA((3, 4)),
            pltpu.SemaphoreType.DMA((3, 4)),
        ],
    )(*grads)
    return tuple(grad[None] for grad in settled)


def settle_copies(*refs):
    held, came, went = refs[6:]
    part = held.shape[1] // 4
    pieces = [(i, k, pl.ds(k * part, part)) for i in range(3) for k in range(4)]
    into = [
        pltpu.make_async_copy(refs[i].at[rows, :], held.at[i, rows, :], came.at[i, k])
        for i, k, rows in pieces
    ]
    out = [
        pltpu.make_async_copy(held.at[i, rows, :], refs[i + 3].at[rows, :], went.at[i, k])
        for i, k, rows in pieces
    ]
    for copy in into:
        copy.start()
    for arrived, copy in zip(into, out):
        arrived.wait()
        copy.start()
    for copy in out:
        copy.wait()


def solution(mesh):
    torus = Mesh(
        mesh.devices.reshape(4, 4, 2, mesh.shape["tensor"]), ("dp_0", "dp_1", "dp_2", "tensor")
    )
    return on_torus(torus)


def on_torus(torus):
    in_specs = (
        P(DP, "tensor", None),
        P(DP, "tensor", None),
        P(),
        P(DP),
        P(DP, "tensor"),
        P(None, "tensor"),
        P(DP, "tensor", None),
        P(DP, "tensor", None),
        P(DP, "tensor", None),
    )
    out_specs = (P(DP, "tensor", None), P(DP, "tensor", None), P(DP, "tensor", None))
    return jax.shard_map(local, mesh=torus, in_specs=in_specs, out_specs=out_specs, check_vma=False)
```
